32 devices in a mesh: ctx: 8 (over y, x, core), fsdp: 4 (over z).
Axes of the slice: x: 2, y: 2, z: 4, core: 2. Of those that a mesh axis runs over, the one named last changes fastest.
Arguments:
- tokens: bfloat16 [4, 2048, 1536], P('fsdp', 'ctx'), may hold values from -6 to 6
- cotangent: bfloat16 [4, 2048, 1536], P('fsdp', 'ctx'), may hold values from -6 to 6
- attend_gain: bfloat16 [1536], P('fsdp'), may hold values from 0.5 to 1.5
- w_query: bfloat16 [1536, 1536], P('fsdp'), may hold values from -0.21875 to 0.21875
- w_key: bfloat16 [1536, 768], P('fsdp'), may hold values from -0.15625 to 0.15625
- w_value: bfloat16 [1536, 768], P('fsdp'), may hold values from -0.15625 to 0.15625
- w_out: bfloat16 [1536, 1536], P('fsdp'), may hold values from -2 to 2
- feed_gain: bfloat16 [1536], P('fsdp'), may hold values from 0.5 to 1.5
- w_gate: bfloat16 [1536, 4096], P('fsdp'), may hold values from -0.15625 to 0.15625
- w_up: bfloat16 [1536, 4096], P('fsdp'), may hold values from -0.15625 to 0.15625
- w_down: bfloat16 [4096, 1536], P('fsdp'), may hold values from -0.1875 to 0.1875
- lengths: int32 [4], P('fsdp'), may hold values from 512 to 2048, as said below
- deal_table: int32 [16], replicated, may hold values from 0 to 15, as said below
Outputs:
- layer_out: bfloat16 [4, 2048, 1536], P('fsdp', 'ctx')
- grad_tokens: float32 [4, 2048, 1536], P('fsdp', 'ctx')
- grad_attend_gain: float32 [1536], P('fsdp')
- grad_query: float32 [1536, 1536], P('fsdp')
- grad_key: float32 [1536, 768], P('fsdp')
- grad_value: float32 [1536, 768], P('fsdp')
- grad_out: float32 [1536, 1536], P('fsdp')
- grad_feed_gain: float32 [1536], P('fsdp')
- grad_gate: float32 [1536, 4096], P('fsdp')
- grad_up: float32 [1536, 4096], P('fsdp')
- grad_down: float32 [4096, 1536], P('fsdp')
- rms_stats: float32 [4, 3], P('fsdp')
The draws below stay inside these ranges and needn't reach their ends.
Inputs may be any that keep to these rules, and one draw needn't show every extreme that they name: Slot s holds valid tokens at sequence positions 0 to lengths[s] - 1, the rest is padding; in every draw some slot is full with 2048. Stored block b of every slot holds the tokens of sequence block deal_table[b]; the table is a permutation, and entries 2c and 2c + 1 sum to 15.
All inputs are finite; a program needn't handle non-finite values.
Results may differ from the reference program's by a relative error of at most 0.015.
Values may be sent and summed in bfloat16 or wider, within the bound.
No kernel may reach another device: no remote copies, remote signals or barrier semaphores. Data moves between devices by JAX's collectives and lax.ppermute only.
A program may use at most 320 MiB of HBM per device.

```python
import math
from functools import partial
import jax
import jax.numpy as jnp
from jax import lax

D = 1536
QUERY_HEADS = 16
KEY_VALUE_HEADS = 8
HEAD_WIDTH = 96
FF = 4096
BLK = 128
KVW = 768
NBLK = 16
SLOT_LENGTH = 2048
SLOTS = 4


def draw_lengths(key, part):
    drawn = jax.random.randint(jax.random.fold_in(key, 11), (SLOTS,), SLOT_LENGTH // 4, SLOT_LENGTH + 1, dtype=jnp.int32)
    chosen = jax.random.randint(jax.random.fold_in(key, 12), (), 0, SLOTS, dtype=jnp.int32)
    return jnp.where(jnp.arange(SLOTS, dtype=jnp.int32) == chosen, SLOT_LENGTH, drawn).astype(jnp.int32)


def draw_deal_table(key, part):
    order = jax.random.permutation(jax.random.fold_in(key, 21), NBLK // 2).astype(jnp.int32)
    return jnp.stack([order, NBLK - 1 - order], axis=1).reshape(NBLK).astype(jnp.int32)


def shard_levels(own_key, extent, split, low, top_value):
    gain = 1.0
    for dim, parts in split:
        heights = jax.random.uniform(jax.random.fold_in(jax.random.fold_in(own_key, 6), dim), (parts,), jnp.float32, low / len(split), top_value / len(split))
        gain = gain * jnp.repeat(jnp.exp(heights), extent[dim] // parts).reshape((-1,) + (1,) * (len(extent) - 1 - dim))
    return gain


def normal_values(rng, extent, scale, most, split=(), held_as=jnp.bfloat16):
    gain = shard_levels(rng, extent, split, -0.22, 0.18) if split else 1.0
    entries = jax.random.normal(rng, extent, jnp.float32) * scale * gain
    return jnp.minimum(jnp.maximum(entries, -most), most).astype(held_as)


def setup_inputs(seed: int = 0) -> dict:
    seeds = jax.random.split(jax.random.key(seed), 14)
    return {
        "tokens": normal_values(seeds[0], (SLOTS, SLOT_LENGTH, D), 1.0, 6.0, ((0, 4), (1, 8))),
        "cotangent": normal_values(seeds[1], (SLOTS, SLOT_LENGTH, D), 1.0, 6.0, ((0, 4), (1, 8))),
        "attend_gain": jnp.clip(1.0 + 0.1 * jax.random.normal(seeds[2], (D,), jnp.float32), 0.5, 1.5).astype(jnp.bfloat16),
        "w_query": normal_values(seeds[3], (D, D), (D // 2) ** -0.5, 0.21875, ((0, 4),)),
        "w_key": normal_values(seeds[4], (D, KVW), D ** -0.5, 0.15625, ((0, 4),)),
        "w_value": normal_values(seeds[5], (D, KVW), D ** -0.5, 0.15625, ((0, 4),)),
        "w_out": normal_values(seeds[6], (D, D), 8 ** -0.5, 2.0, ((0, 4),)),
        "feed_gain": jnp.clip(1.0 + 0.1 * jax.random.normal(seeds[7], (D,), jnp.float32), 0.5, 1.5).astype(jnp.bfloat16),
        "w_gate": normal_values(seeds[8], (D, FF), D ** -0.5, 0.15625, ((0, 4),)),
        "w_up": normal_values(seeds[9], (D, FF), D ** -0.5, 0.15625, ((0, 4),)),
        "w_down": normal_values(seeds[10], (FF, D), (FF // 4) ** -0.5, 0.1875, ((0, 4),)),
        "lengths": draw_lengths(jax.random.fold_in(seeds[13], 71), 0),
        "deal_table": draw_deal_table(jax.random.fold_in(seeds[13], 71), 0),
    }


EPS = 1e-05
ROPE_BASE = 10000.0
NEG = -1e+30
HIGHEST = lax.Precision.HIGHEST

@jax.custom_vjp
def reduced_copy(v):
    return lax.optimization_barrier(v.astype(jnp.bfloat16)).astype(jnp.float32)

@jax.custom_vjp
def low_back(v):
    return v

def low_keep(v):
    return (reduced_copy(v), None)

def low_pass(kept, grad):
    return (grad,)

def back_keep(v):
    return (v, None)

def back_low(kept, grad):
    return (reduced_copy(grad),)
reduced_copy.defvjp(low_keep, low_pass)
low_back.defvjp(back_keep, back_low)

def matmul_high(left, right):
    return jnp.dot(left, right, precision=HIGHEST, preferred_element_type=jnp.float32)

def norm_rows(residual, scale_gain):
    return residual * lax.rsqrt(lax.optimization_barrier(jnp.mean(residual * residual, axis=-1, keepdims=True)) + EPS) * scale_gain

def apply_rotation(value_rows, cosine_table, sine_table):
    half_width = value_rows.shape[-1] // 2
    lead_half = value_rows[..., :half_width]
    tail_half = value_rows[..., half_width:]
    return jnp.concatenate([lead_half * cosine_table - tail_half * sine_table, tail_half * cosine_table + lead_half * sine_table], axis=-1)

def attend(operands, allowed):
    query_h, key_h, value_h = operands
    scores = low_back(jnp.einsum('gqd,kd->gqk', query_h, key_h, precision=HIGHEST) * (1.0 / math.sqrt(HEAD_WIDTH)))
    scores = jnp.where(allowed[None], scores, NEG)
    row_top = lax.optimization_barrier(jnp.max(scores, axis=-1, keepdims=True))
    shifted = jnp.exp(scores - row_top)
    soft_low = reduced_copy(shifted / lax.optimization_barrier(jnp.sum(shifted, axis=-1, keepdims=True)))
    return jnp.einsum('gqk,kd->gqd', soft_low, value_h, precision=HIGHEST)

def block_forward(residual, weight_set, allowed, live_rows, cosine_table, sine_table):
    attend_gain, w_query, w_key, w_value, w_out, feed_gain, w_gate, w_up, w_down = weight_set
    group_count = QUERY_HEADS // KEY_VALUE_HEADS
    attend_in = reduced_copy(norm_rows(residual, attend_gain))
    query_raw = low_back(matmul_high(attend_in, w_query))
    key_unrotated = low_back(matmul_high(attend_in, w_key))
    value_reduced = reduced_copy(low_back(matmul_high(attend_in, w_value)))
    query_reduced = reduced_copy(apply_rotation(query_raw.reshape(SLOT_LENGTH, QUERY_HEADS, HEAD_WIDTH), cosine_table, sine_table))
    key_reduced = reduced_copy(apply_rotation(key_unrotated.reshape(SLOT_LENGTH, KEY_VALUE_HEADS, HEAD_WIDTH), cosine_table, sine_table))
    query_head_rows = query_reduced.reshape(SLOT_LENGTH, KEY_VALUE_HEADS, group_count, HEAD_WIDTH).transpose(1, 2, 0, 3)
    key_heads = key_reduced.transpose(1, 0, 2)
    value_head_rows = value_reduced.reshape(SLOT_LENGTH, KEY_VALUE_HEADS, HEAD_WIDTH).transpose(1, 0, 2)
    context = lax.map(jax.checkpoint(partial(attend, allowed=allowed)), (query_head_rows, key_heads, value_head_rows))
    context_low = low_back(reduced_copy(context.transpose(2, 0, 1, 3).reshape(SLOT_LENGTH, QUERY_HEADS * HEAD_WIDTH)))
    attend_branch = low_back(matmul_high(context_low, w_out))
    middle = residual + attend_branch
    feed_in = reduced_copy(norm_rows(middle, feed_gain))
    gate_pre = low_back(matmul_high(feed_in, w_gate))
    up_pre = low_back(matmul_high(feed_in, w_up))
    hidden_low = reduced_copy(jax.nn.silu(gate_pre) * up_pre)
    feed_branch = low_back(matmul_high(hidden_low, w_down))
    final_sum = middle + feed_branch
    return (final_sum * live_rows, (final_sum, attend_branch, feed_branch))

def reference(tokens, cotangent, attend_gain, w_query, w_key, w_value, w_out, feed_gain, w_gate, w_up, w_down, lengths, deal_table):
    weight_set = (attend_gain.astype(jnp.float32), w_query.astype(jnp.float32), w_key.astype(jnp.float32), w_value.astype(jnp.float32), w_out.astype(jnp.float32), feed_gain.astype(jnp.float32), w_gate.astype(jnp.float32), w_up.astype(jnp.float32), w_down.astype(jnp.float32))
    within = jnp.arange(BLK, dtype=jnp.int32)
    pos_all = (deal_table[:, None] * BLK + within[None, :]).reshape(-1).astype(jnp.int32)
    frequency = ROPE_BASE ** (-2.0 * jnp.arange(HEAD_WIDTH // 2, dtype=jnp.float32) / HEAD_WIDTH)
    angles = pos_all.astype(jnp.float32)[:, None] * frequency[None, :]
    cosine_table = jnp.cos(angles)[:, None, :]
    sine_table = jnp.sin(angles)[:, None, :]

    def per_slot(running, inputs):
        slot_tokens, slot_cot, length = inputs
        allowed = (pos_all[None, :] <= pos_all[:, None]) & (pos_all[None, :] < length)
        live_rows = (pos_all < length).astype(jnp.float32)[:, None]

        def forward(residual, weights_in):
            return block_forward(residual, weights_in, allowed, live_rows, cosine_table, sine_table)
        slot_out, pullback, branches = jax.vjp(forward, slot_tokens.astype(jnp.float32), weight_set, has_aux=True)
        grad_resid, grad_weights = pullback(slot_cot.astype(jnp.float32))
        running = tuple((before + piece_grad for before, piece_grad in zip(running, grad_weights)))
        token_count = length.astype(jnp.float32) * D
        slot_stats = jnp.stack([jnp.sqrt(jnp.sum(branch * branch * live_rows) / token_count) for branch in branches])
        return (running, (slot_out.astype(jnp.bfloat16), grad_resid, slot_stats))
    zero_grads = tuple((jnp.zeros(weight.shape, jnp.float32) for weight in weight_set))
    totals, (layer_out, grad_tokens, rms_stats) = lax.scan(per_slot, zero_grads, (tokens, cotangent, lengths))
    return (layer_out, grad_tokens, totals[0], totals[1], totals[2], totals[3], totals[4], totals[5], totals[6], totals[7], totals[8], rms_stats)
```

```python
import functools
import math

import jax
import jax.numpy as jnp
from jax import lax
from jax.experimental import pallas as pl
from jax.experimental.pallas import tpu as pltpu
from jax.sharding import PartitionSpec as P

D = 1536
QUERY_HEADS = 16
KEY_VALUE_HEADS = 8
HEAD_WIDTH = 96
HALF = HEAD_WIDTH // 2
BLK = 128
LANES = 128

EPS = 1e-05
ROPE_BASE = 10000.0
NEG = -1e30
SCALE = 1.0 / math.sqrt(HEAD_WIDTH)
TILE = 256
CHUNKS = 4

F32 = jnp.float32
BF16 = jnp.bfloat16


def dot(left, right):
    return lax.dot_general(left, right, (((1,), (0,)), ((), ())), preferred_element_type=F32)


def dot_t(left, right):
    return lax.dot_general(left, right, (((1,), (1,)), ((), ())), preferred_element_type=F32)


def dot_outer(left, right):
    return lax.dot_general(left, right, (((0,), (0,)), ((), ())), preferred_element_type=F32)


def turn(rows, cos_rows, sin_rows):
    return rows * cos_rows + pltpu.roll(rows, LANES // 2, 1) * sin_rows


def mask_tile(scores, key_start, query_start, length):
    key_pos = key_start + lax.broadcasted_iota(jnp.int32, scores.shape, 0)
    query_pos = query_start + lax.broadcasted_iota(jnp.int32, scores.shape, 1)
    return jnp.where((key_pos <= query_pos) & (key_pos < length), scores, NEG)


def attend_kernel(
    heads, table, length_ref, raw, cos_t, sin_t, ctx_low, query_s, key_s, value_s, ctx_s, lse_s,
    score_s,
):
    rows_all = raw.shape[0]
    length = length_ref[0]

    @pl.loop(0, rows_all // BLK)
    def _(b):
        src = pl.ds(pl.multiple_of(b * BLK, BLK), BLK)
        dst = pl.ds(pl.multiple_of(table[b] * BLK, BLK), BLK)
        cos_rows = cos_t[src, :]
        sin_rows = sin_t[src, :]
        for h in range(heads):
            part = raw[src, h * LANES : (h + 1) * LANES]
            query_s[h, dst, :] = turn(part, cos_rows, sin_rows).astype(BF16)
        part = raw[src, heads * LANES : (heads + 1) * LANES]
        key_s[dst, :] = turn(part, cos_rows, sin_rows).astype(BF16)
        value_s[dst, :] = raw[src, (heads + 1) * LANES : (heads + 2) * LANES].astype(BF16)

    @pl.loop(0, rows_all // TILE)
    def _(i):
        q_rows = pl.ds(pl.multiple_of(i * TILE, TILE), TILE)
        full = jnp.minimum(i, length // TILE)
        for h in range(heads):
            query = query_s[h, q_rows, :]

            def score(j, top, masked):
                k_rows = pl.ds(pl.multiple_of(j * TILE, TILE), TILE)
                tile = dot_t(key_s[k_rows, :], query)
                if masked:
                    tile = mask_tile(tile, j * TILE, i * TILE, length)
                score_s[k_rows, :] = tile
                return jnp.maximum(top, jnp.max(tile, axis=0, keepdims=True))

            top = jnp.full((1, TILE), NEG, F32)
            top = lax.fori_loop(0, full, lambda j, t: score(j, t, False), top)
            top = lax.fori_loop(full, i + 1, lambda j, t: score(j, t, True), top)

            def accumulate(j, carry):
                total, context = carry
                k_rows = pl.ds(pl.multiple_of(j * TILE, TILE), TILE)
                weight = jnp.exp((score_s[k_rows, :] - top) * SCALE)
                total = total + jnp.sum(weight, axis=0, keepdims=True)
                context = context + dot_outer(value_s[k_rows, :], weight.astype(BF16))
                return total, context

            total, context = lax.fori_loop(
                0, i + 1, accumulate, (jnp.zeros((1, TILE), F32), jnp.zeros((LANES, TILE), F32))
            )
            ctx_s[q_rows, h * LANES : (h + 1) * LANES] = (context / total).T
            lse_s[h, :, q_rows] = jnp.broadcast_to(top * SCALE + jnp.log(total), (8, TILE))

    @pl.loop(0, rows_all // BLK)
    def _(b):
        dst = pl.ds(pl.multiple_of(b * BLK, BLK), BLK)
        src = pl.ds(pl.multiple_of(table[b] * BLK, BLK), BLK)
        ctx_low[dst, :] = ctx_s[src, :].astype(BF16)


def attend(table, length, raw, cos_t, sin_t, heads):
    rows_all = raw.shape[0]
    smem = pl.BlockSpec(memory_space=pltpu.SMEM)
    vmem = pl.BlockSpec(memory_space=pltpu.VMEM)
    pairs = heads * rows_all * rows_all // 2
    return pl.pallas_call(
        functools.partial(attend_kernel, heads),
        out_shape=(
            jax.ShapeDtypeStruct((rows_all, heads * LANES), BF16),
            jax.ShapeDtypeStruct((heads, rows_all, LANES), BF16),
            jax.ShapeDtypeStruct((rows_all, LANES), BF16),
            jax.ShapeDtypeStruct((rows_all, LANES), BF16),
            jax.ShapeDtypeStruct((rows_all, heads * LANES), F32),
            jax.ShapeDtypeStruct((heads, 8, rows_all), F32),
        ),
        in_specs=[smem, smem, vmem, vmem, vmem],
        out_specs=(vmem,) * 6,
        scratch_shapes=[pltpu.VMEM((rows_all, TILE), F32)],
        compiler_params=pltpu.CompilerParams(vmem_limit_bytes=48 << 20),
        cost_estimate=pl.CostEstimate(
            flops=4 * pairs * LANES, transcendentals=pairs, bytes_accessed=rows_all * 8192
        ),
        name="attend",
    )(table, length, raw, cos_t, sin_t)


def attend_back_kernel(
    heads, table, length_ref, query_s, key_s, value_s, ctx_s, lse_s, back_low, cos_t, sin_t, out,
    back_s, delta_s, query_acc, key_all, value_all,
):
    rows_all = key_s.shape[0]
    length = length_ref[0]
    tiles = rows_all // TILE

    @pl.loop(0, rows_all // BLK)
    def _(b):
        src = pl.ds(pl.multiple_of(b * BLK, BLK), BLK)
        dst = pl.ds(pl.multiple_of(table[b] * BLK, BLK), BLK)
        for h in range(heads):
            cols = slice(h * LANES, (h + 1) * LANES)
            part = back_low[src, cols]
            back_s[h, dst, :] = part
            inner = jnp.sum(part.astype(F32) * ctx_s[dst, cols], axis=1, keepdims=True)
            delta_s[h, :, dst] = jnp.broadcast_to(inner, (BLK, BLK)).T[:8, :]

    query_acc[...] = jnp.zeros_like(query_acc)
    key_all[...] = jnp.zeros_like(key_all)
    value_all[...] = jnp.zeros_like(value_all)

    def step(i, j, masked):
        k_rows = pl.ds(pl.multiple_of(j * TILE, TILE), TILE)
        q_rows = pl.ds(pl.multiple_of(i * TILE, TILE), TILE)
        key = key_s[k_rows, :]
        value = value_s[k_rows, :]
        value_sum = key_sum = None
        for h in range(heads):
            query = query_s[h, q_rows, :]
            back = back_s[h, q_rows, :]
            tile = dot_t(key, query)
            if masked:
                tile = mask_tile(tile, j * TILE, i * TILE, length)
            soft = jnp.exp(tile * SCALE - lse_s[h, :1, q_rows])
            back_soft = dot_t(value, back)
            low = (soft * (back_soft - delta_s[h, :1, q_rows])).astype(BF16)
            value_part = dot(soft.astype(BF16), back)
            key_part = dot(low, query)
            value_sum = value_part if h == 0 else value_sum + value_part
            key_sum = key_part if h == 0 else key_sum + key_part
            query_acc[h, q_rows, :] += dot_outer(low, key)
        value_all[k_rows, :] += value_sum
        key_all[k_rows, :] += key_sum

    @pl.loop(0, tiles)
    def _(i):
        full = jnp.minimum(i, length // TILE)

        @pl.loop(0, full)
        def _(j):
            step(i, j, False)

        @pl.loop(full, i + 1)
        def _(j):
            step(i, j, True)

    @pl.loop(0, rows_all // BLK)
    def _(b):
        dst = pl.ds(pl.multiple_of(b * BLK, BLK), BLK)
        src = pl.ds(pl.multiple_of(table[b] * BLK, BLK), BLK)
        cos_rows = cos_t[dst, :]
        sin_rows = -sin_t[dst, :]
        for h in range(heads):
            part = query_acc[h, src, :] * SCALE
            out[dst, h * LANES : (h + 1) * LANES] = turn(part, cos_rows, sin_rows).astype(BF16)
        part = key_all[src, :] * SCALE
        out[dst, heads * LANES : (heads + 1) * LANES] = turn(part, cos_rows, sin_rows).astype(BF16)
        out[dst, (heads + 1) * LANES : (heads + 2) * LANES] = value_all[src, :].astype(BF16)


def attend_back(table, length, saved, back_low, cos_t, sin_t, heads):
    query_s, key_s, value_s, ctx_s, lse_s = saved
    rows_all = key_s.shape[0]
    smem = pl.BlockSpec(memory_space=pltpu.SMEM)
    vmem = pl.BlockSpec(memory_space=pltpu.VMEM)
    pairs = heads * rows_all * rows_all // 2
    return pl.pallas_call(
        functools.partial(attend_back_kernel, heads),
        out_shape=jax.ShapeDtypeStruct((rows_all, (heads + 2) * LANES), BF16),
        in_specs=[smem, smem] + [vmem] * 8,
        out_specs=vmem,
        scratch_shapes=[
            pltpu.VMEM((heads, rows_all, LANES), BF16),
            pltpu.VMEM((heads, 8, rows_all), F32),
            pltpu.VMEM((heads, rows_all, LANES), F32),
            pltpu.VMEM((rows_all, LANES), F32),
            pltpu.VMEM((rows_all, LANES), F32),
        ],
        compiler_params=pltpu.CompilerParams(vmem_limit_bytes=48 << 20),
        cost_estimate=pl.CostEstimate(
            flops=10 * pairs * LANES, transcendentals=pairs, bytes_accessed=rows_all * 8192
        ),
        name="attend_back",
    )(table, length, query_s, key_s, value_s, ctx_s, lse_s, back_low, cos_t, sin_t)


def hop(value, size, bit):
    return lax.ppermute(value, "ctx", [(i, i ^ bit) for i in range(size)])


def gather_rows(block, size):
    if size != 8:
        return jnp.split(lax.all_gather(block, "ctx", axis=0, tiled=True), CHUNKS)
    half = block.shape[0] // 2
    across = hop(block, size, 2)
    along = hop(block, size, 4)
    upper = hop(along[:half], size, 2)
    lower = hop(across[half:], size, 4)
    corner = jnp.concatenate([upper, lower])
    return [jnp.concatenate([part, hop(part, size, 1)]) for part in (block, across, along, corner)]


def scatter_rows(make, size):
    if size != 8:
        whole = jnp.concatenate([make(k) for k in range(CHUNKS)]).astype(BF16)
        return lax.psum_scatter(whole, "ctx", scatter_dimension=0, tiled=True).astype(F32)

    def fold(k):
        piece = make(k)
        rows = piece.shape[0] // 2
        return piece[:rows] + hop(piece[rows:].astype(BF16), size, 1).astype(F32)

    corner, across, along, own = fold(3), fold(1), fold(2), fold(0)
    half = own.shape[0] // 2

    def send(value, bit):
        return hop(value.astype(BF16), size, bit).astype(F32)

    for_along = send(corner[:half], 2)
    for_across = send(corner[half:], 4)
    across_top = send(across[:half], 2)
    along_low = send(along[half:], 4)
    across_low = send(across[half:] + for_across, 2)
    along_top = send(along[:half] + for_along, 4)
    return jnp.concatenate(
        [own[:half] + across_top + along_top, own[half:] + across_low + along_low]
    )


def norm_back(residual, scale_rows, gain, upstream):
    weighted = upstream * gain
    row_inner = jnp.mean(weighted * residual, axis=-1, keepdims=True)
    return scale_rows * weighted - residual * (scale_rows * scale_rows * scale_rows) * row_inner


def pad_turned(weight):
    rows, cols = weight.shape
    split = weight.reshape(rows, cols // HALF, HALF)
    return jnp.pad(split, ((0, 0), (0, 0), (0, LANES // 2 - HALF))).reshape(rows, -1)


def drop_turned(grad):
    rows, cols = grad.shape
    return grad.reshape(rows, cols * 2 // LANES, LANES // 2)[:, :, :HALF].reshape(rows, -1)


def local(
    size,
    planes,
    tokens,
    cotangent,
    attend_gain,
    w_query,
    w_key,
    w_value,
    w_out,
    feed_gain,
    w_gate,
    w_up,
    w_down,
    lengths,
    deal_table,
):
    me = lax.axis_index("ctx")
    plane = lax.axis_index("fsdp")
    rows_here = tokens.shape[1]
    rows_all = rows_here * size
    heads = QUERY_HEADS // size
    shares = max(1, size // KEY_VALUE_HEADS)
    shard = w_query.shape[0]
    ff = w_gate.shape[1]
    ff_mine = ff // planes // size
    q_cols = heads * HEAD_WIDTH
    key_head = me // shares

    query_cut = lax.dynamic_slice_in_dim(w_query, me * q_cols, q_cols, 1)
    key_cut = lax.dynamic_slice_in_dim(w_key, key_head * HEAD_WIDTH, HEAD_WIDTH, 1)
    value_cut = lax.dynamic_slice_in_dim(w_value, key_head * HEAD_WIDTH, HEAD_WIDTH, 1)
    proj_cut = jnp.concatenate([query_cut, key_cut, value_cut], axis=1)
    cut_cols = proj_cut.shape[1]
    gains = jnp.zeros((16, cut_cols), BF16)
    gains = gains.at[0, :shard].set(attend_gain).at[1, :shard].set(feed_gain)
    proj_all = lax.all_gather(jnp.concatenate([proj_cut, gains]), "fsdp", axis=0)
    gain_one = proj_all[:, shard, :shard].reshape(1, D).astype(F32)
    gain_two = proj_all[:, shard + 1, :shard].reshape(1, D).astype(F32)
    proj_all = proj_all[:, :shard].reshape(D, cut_cols)
    proj_w = jnp.concatenate(
        [
            pad_turned(proj_all[:, : q_cols + HEAD_WIDTH]),
            jnp.pad(proj_all[:, q_cols + HEAD_WIDTH :], ((0, 0), (0, LANES - HEAD_WIDTH))),
        ],
        axis=1,
    )

    out_start = me * q_cols
    out_rows = lax.dynamic_slice_in_dim(w_out, lax.rem(out_start, shard), q_cols, 0)
    owns_out = plane == out_start // shard
    out_w = lax.psum(jnp.where(owns_out, out_rows, jnp.zeros_like(out_rows)), "fsdp")
    out_w = jnp.pad(
        out_w.reshape(heads, HEAD_WIDTH, D), ((0, 0), (0, LANES - HEAD_WIDTH), (0, 0))
    ).reshape(heads * LANES, D)

    def ff_cut(weight):
        split = weight.reshape(shard, planes, size, ff_mine)
        return lax.dynamic_slice_in_dim(split, me, 1, 2).reshape(shard, planes * ff_mine)

    ff_cols = planes * ff_mine
    pair_w = lax.all_gather(
        jnp.concatenate([ff_cut(w_gate), ff_cut(w_up)], axis=1), "fsdp", axis=0, tiled=True
    )
    gate_w, up_w = pair_w[:, :ff_cols], pair_w[:, ff_cols:]
    down_w = lax.all_gather(
        lax.dynamic_slice_in_dim(w_down, me * ff_mine, ff_mine, 0), "fsdp", axis=0, tiled=True
    )

    order = jnp.arange(size, dtype=jnp.int32)
    if size == 8:
        order = jnp.bitwise_xor(order, me)
    table = deal_table.reshape(size, rows_here // BLK)[order].reshape(-1)
    pos_all = (table[:, None] * BLK + jnp.arange(BLK, dtype=jnp.int32)[None, :]).reshape(-1)
    live_all = (pos_all < lengths[0]).astype(F32)[:, None]
    if size == 8:
        live = live_all[:rows_here]
    else:
        live = lax.dynamic_slice_in_dim(live_all, me * rows_here, rows_here)
    frequency = ROPE_BASE ** (-2.0 * jnp.arange(HALF, dtype=F32) / HEAD_WIDTH)
    angles = pos_all.astype(F32)[:, None] * frequency[None, :]
    pad = jnp.zeros((rows_all, LANES // 2 - HALF), F32)
    cosine, sine = jnp.cos(angles), jnp.sin(angles)
    cos_t = jnp.concatenate([cosine, pad, cosine, pad], axis=1)
    sin_t = jnp.concatenate([-sine, pad, sine, pad], axis=1)

    residual = tokens[0].astype(F32)
    token_parts = gather_rows(tokens[0], size)

    def norm(rows, gain):
        scale_rows = lax.rsqrt(jnp.mean(rows * rows, axis=-1, keepdims=True) + EPS)
        return rows * scale_rows * gain, scale_rows

    _, scale_one = norm(residual, gain_one)
    attend_parts = [norm(part.astype(F32), gain_one)[0].astype(BF16) for part in token_parts]
    raw = jnp.concatenate([dot(part, proj_w) for part in attend_parts])
    ctx_low, *saved = attend(table, lengths, raw, cos_t, sin_t, heads)
    piece = rows_all // CHUNKS

    def part_of(array, k):
        return array[k * piece : (k + 1) * piece]

    attend_branch = scatter_rows(lambda k: dot(part_of(ctx_low, k), out_w), size)
    middle = residual + attend_branch

    back_parts_in = gather_rows(cotangent[0], size)
    back_low = [
        (part.astype(F32) * part_of(live_all, k)).astype(BF16)
        for k, part in enumerate(back_parts_in)
    ]
    normed_two, scale_two = norm(middle, gain_two)
    feed_parts = gather_rows(normed_two.astype(BF16), size)
    hidden_parts, gate_back_parts, up_back_parts = [], [], []
    for k in range(CHUNKS):
        gate_pre = dot(feed_parts[k], gate_w)
        up_pre = dot(feed_parts[k], up_w)
        gate_sigmoid = jax.nn.sigmoid(gate_pre)
        gate_silu = gate_pre * gate_sigmoid
        hidden_parts.append((gate_silu * up_pre).astype(BF16))
        back_hidden = dot_t(back_low[k], down_w)
        gate_back_parts.append(
            (
                back_hidden * up_pre * gate_sigmoid * (1.0 + gate_pre * (1.0 - gate_sigmoid))
            ).astype(BF16)
        )
        up_back_parts.append((back_hidden * gate_silu).astype(BF16))
    back_feed_in = scatter_rows(
        lambda k: dot_t(gate_back_parts[k], gate_w) + dot_t(up_back_parts[k], up_w), size
    )
    back_final = cotangent[0].astype(F32) * live
    back_middle = back_final + norm_back(middle, scale_two, gain_two, back_feed_in)
    gain_two_grad = jnp.sum(back_feed_in * middle * scale_two, axis=0)

    feed_branch = scatter_rows(lambda k: dot(hidden_parts[k], down_w), size)
    final_sum = middle + feed_branch
    layer_out = (final_sum * live).astype(BF16)
    sums = jnp.stack(
        [
            jnp.sum(final_sum * final_sum * live),
            jnp.sum(attend_branch * attend_branch * live),
            jnp.sum(feed_branch * feed_branch * live),
        ]
    )

    feed_all = jnp.concatenate(feed_parts)
    hidden_all = jnp.concatenate(hidden_parts)
    back_all = jnp.concatenate(back_low)
    pair_back = jnp.concatenate(
        [
            jnp.concatenate([g, u], axis=1)
            for g, u in zip(gate_back_parts, up_back_parts)
        ]
    )
    pair_grad = dot_outer(feed_all, pair_back).astype(BF16)
    down_grad = dot_outer(hidden_all, back_all).astype(BF16)
    pair_grad = lax.psum_scatter(pair_grad, "fsdp", scatter_dimension=0, tiled=True)
    down_grad = lax.psum_scatter(down_grad, "fsdp", scatter_dimension=0, tiled=True)
    pair_grad = lax.all_gather(pair_grad, "ctx", axis=0)
    grad_down = lax.all_gather(down_grad, "ctx", axis=0, tiled=True).astype(F32)
    pair_grad = (
        pair_grad.reshape(size, shard, 2, planes, ff_mine)
        .transpose(2, 1, 3, 0, 4)
        .reshape(2, shard, ff)
        .astype(F32)
    )
    grad_gate, grad_up = pair_grad[0], pair_grad[1]

    mid_parts = gather_rows(back_middle.astype(BF16), size)
    back_context = jnp.concatenate([dot_t(part, out_w) for part in mid_parts]).astype(BF16)
    turned = attend_back(table, lengths, saved, back_context, cos_t, sin_t, heads)
    if shares > 1:
        pairs = [[g * shares + i for i in range(shares)] for g in range(size // shares)]
        both = lax.psum(turned[:, heads * LANES :].astype(F32), "ctx", axis_index_groups=pairs)
        first = (lax.rem(me, shares) == 0).astype(F32)
        turned = jnp.concatenate([turned[:, : heads * LANES], (both * first).astype(BF16)], axis=1)

    mid_all = jnp.concatenate(mid_parts)
    out_grad = dot_outer(ctx_low, mid_all).reshape(heads, LANES, D)[:, :HEAD_WIDTH]
    out_grad = lax.psum(out_grad.reshape(q_cols, D).astype(BF16), "fsdp")
    placed = jnp.zeros((shard, D), BF16)
    placed = lax.dynamic_update_slice_in_dim(
        placed, jnp.where(owns_out, out_grad, jnp.zeros_like(out_grad)),
        lax.rem(out_start, shard), 0,
    )
    out_piece = lax.psum_scatter(placed, "ctx", scatter_dimension=0, tiled=True)

    back_in = [dot_t(part_of(turned, k), proj_w) for k in range(CHUNKS)]
    back_attend_in = scatter_rows(lambda k: back_in[k], size)
    grad_tokens = back_middle + norm_back(residual, scale_one, gain_one, back_attend_in)
    gain_one_grad = jnp.sum(back_attend_in * residual * scale_one, axis=0)

    attend_all = jnp.concatenate(attend_parts)
    proj_grad = dot_outer(attend_all, turned)
    turn_cols = (heads + 1) * LANES
    proj_grad = jnp.concatenate(
        [
            drop_turned(proj_grad[:, :turn_cols]),
            proj_grad[:, turn_cols : turn_cols + HEAD_WIDTH],
        ],
        axis=1,
    ).astype(BF16)
    proj_grad = lax.psum_scatter(proj_grad, "fsdp", scatter_dimension=0, tiled=True)
    proj_grad = lax.all_gather(proj_grad, "ctx", axis=0).astype(F32)
    grad_query = proj_grad[:, :, :q_cols].transpose(1, 0, 2).reshape(shard, D)

    def key_columns(start):
        cols = proj_grad[::shares, :, start : start + HEAD_WIDTH]
        return cols.transpose(1, 0, 2).reshape(shard, KEY_VALUE_HEADS * HEAD_WIDTH)

    grad_key = key_columns(q_cols)
    grad_value = key_columns(q_cols + HEAD_WIDTH)
    grad_out = lax.all_gather(out_piece, "ctx", axis=0, tiled=True).astype(F32)

    slot = (jnp.arange(planes) == plane).astype(F32)
    stats = jnp.pad(slot[:, None] * sums[None, :], ((0, 0), (0, LANES - 3))).reshape(-1)
    small = lax.psum(
        jnp.concatenate([gain_one_grad, gain_two_grad, stats]), ("ctx", "fsdp")
    )
    grad_attend_gain = lax.dynamic_slice_in_dim(small[:D], plane * shard, shard)
    grad_feed_gain = lax.dynamic_slice_in_dim(small[D : 2 * D], plane * shard, shard)
    total_sums = lax.dynamic_slice_in_dim(small[2 * D :].reshape(planes, LANES), plane, 1)[:, :3]
    rms_stats = jnp.sqrt(total_sums / (lengths.astype(F32)[:, None] * D))
    return (
        layer_out[None],
        grad_tokens[None],
        grad_attend_gain,
        grad_query,
        grad_key,
        grad_value,
        grad_out,
        grad_feed_gain,
        grad_gate,
        grad_up,
        grad_down,
        rms_stats,
    )


def solution(mesh):
    rows = P("fsdp", "ctx", None)
    vector = P("fsdp")
    matrix = P("fsdp", None)
    in_specs = (rows, rows, vector, matrix, matrix, matrix, matrix, vector, matrix, matrix, matrix)
    in_specs += (vector, P())
    out_specs = (rows, rows, vector, matrix, matrix, matrix, matrix, vector, matrix, matrix, matrix)
    out_specs += (matrix,)
    body = functools.partial(local, mesh.shape["ctx"], mesh.shape["fsdp"])
    return jax.shard_map(
        body, mesh=mesh, in_specs=in_specs, out_specs=out_specs, check_vma=False
    )
```

```python
import functools
import math

import jax
import jax.numpy as jnp
from jax import lax
from jax.experimental import pallas as pl
from jax.experimental.pallas import tpu as pltpu
from jax.sharding import PartitionSpec as P

D = 1536
QUERY_HEADS = 16
KEY_VALUE_HEADS = 8
HEAD_WIDTH = 96
HALF = HEAD_WIDTH // 2
BLK = 128
LANES = 128

EPS = 1e-05
ROPE_BASE = 10000.0
NEG = -1e30
SCALE = 1.0 / math.sqrt(HEAD_WIDTH)
TILE = 256
CHUNKS = 4

F32 = jnp.float32
BF16 = jnp.bfloat16


def dot(left, right):
    return lax.dot_general(left, right, (((1,), (0,)), ((), ())), preferred_element_type=F32)


def dot_t(left, right):
    return lax.dot_general(left, right, (((1,), (1,)), ((), ())), preferred_element_type=F32)


def dot_outer(left, right):
    return lax.dot_general(left, right, (((0,), (0,)), ((), ())), preferred_element_type=F32)


def turn(rows, cos_rows, sin_rows):
    return rows * cos_rows + pltpu.roll(rows, LANES // 2, 1) * sin_rows


def mask_tile(scores, key_start, query_start, length):
    key_pos = key_start + lax.broadcasted_iota(jnp.int32, scores.shape, 0)
    query_pos = query_start + lax.broadcasted_iota(jnp.int32, scores.shape, 1)
    return jnp.where((key_pos <= query_pos) & (key_pos < length), scores, NEG)


def attend_kernel(heads, table, length_ref, *refs):
    raws, rest = refs[:CHUNKS], refs[CHUNKS:]
    cos_t, sin_t, ctx_low, query_s, key_s, value_s, ctx_s, lse_s, value_t, score_s = rest
    rows_all = key_s.shape[0]
    piece = raws[0].shape[0] // BLK
    length = length_ref[0]

    for k, raw in enumerate(raws):

        @pl.loop(0, piece)
        def _(b, k=k, raw=raw):
            src = pl.ds(pl.multiple_of(b * BLK, BLK), BLK)
            here = pl.ds(pl.multiple_of((k * piece + b) * BLK, BLK), BLK)
            dst = pl.ds(pl.multiple_of(table[k * piece + b] * BLK, BLK), BLK)
            cos_rows = cos_t[here, :]
            sin_rows = sin_t[here, :]
            for h in range(heads):
                part = raw[src, h * LANES : (h + 1) * LANES]
                query_s[h, dst, :] = turn(part, cos_rows, sin_rows).astype(BF16)
            part = raw[src, heads * LANES : (heads + 1) * LANES]
            key_s[dst, :] = turn(part, cos_rows, sin_rows).astype(BF16)
            part = raw[src, (heads + 1) * LANES : (heads + 2) * LANES]
            value_s[dst, :] = part.astype(BF16)
            value_t[:, dst] = part.T.astype(BF16)

    every = range(heads)

    @pl.loop(0, rows_all // TILE)
    def _(i):
        q_rows = pl.ds(pl.multiple_of(i * TILE, TILE), TILE)
        full = jnp.minimum(i, length // TILE)

        def score(j, tops, masked):
            k_rows = pl.ds(pl.multiple_of(j * TILE, TILE), TILE)
            key = key_s[k_rows, :]
            out = []
            for h in every:
                tile = dot_t(key, query_s[h, q_rows, :])
                if masked:
                    tile = mask_tile(tile, j * TILE, i * TILE, length)
                score_s[h, k_rows, :] = tile
                out.append(jnp.maximum(tops[h], jnp.max(tile, axis=0, keepdims=True)))
            return tuple(out)

        tops = tuple(jnp.full((1, TILE), NEG, F32) for _ in every)
        tops = lax.fori_loop(0, full, lambda j, t: score(j, t, False), tops)
        tops = lax.fori_loop(full, i + 1, lambda j, t: score(j, t, True), tops)

        def accumulate(j, carry):
            k_rows = pl.ds(pl.multiple_of(j * TILE, TILE), TILE)
            out = []
            for h in every:
                total, context = carry[h]
                weight = jnp.exp((score_s[h, k_rows, :] - tops[h]) * SCALE)
                total = total + jnp.sum(weight, axis=0, keepdims=True)
                context = context + dot(value_t[:, k_rows], weight.astype(BF16))
                out.append((total, context))
            return tuple(out)

        start = tuple((jnp.zeros((1, TILE), F32), jnp.zeros((LANES, TILE), F32)) for _ in every)
        sums = lax.fori_loop(0, i + 1, accumulate, start)
        for h in every:
            total, context = sums[h]
            ctx_s[q_rows, h * LANES : (h + 1) * LANES] = (context / total).T
            lse_s[h, :, q_rows] = jnp.broadcast_to(tops[h] * SCALE + jnp.log(total), (8, TILE))

    @pl.loop(0, rows_all // BLK)
    def _(b):
        dst = pl.ds(pl.multiple_of(b * BLK, BLK), BLK)
        src = pl.ds(pl.multiple_of(table[b] * BLK, BLK), BLK)
        ctx_low[dst, :] = ctx_s[src, :].astype(BF16)


def attend(table, length, raws, cos_t, sin_t, heads):
    rows_all = cos_t.shape[0]
    smem = pl.BlockSpec(memory_space=pltpu.SMEM)
    vmem = pl.BlockSpec(memory_space=pltpu.VMEM)
    pairs = heads * rows_all * rows_all // 2
    return pl.pallas_call(
        functools.partial(attend_kernel, heads),
        out_shape=(
            jax.ShapeDtypeStruct((rows_all, heads * LANES), BF16),
            jax.ShapeDtypeStruct((heads, rows_all, LANES), BF16),
            jax.ShapeDtypeStruct((rows_all, LANES), BF16),
            jax.ShapeDtypeStruct((rows_all, LANES), BF16),
            jax.ShapeDtypeStruct((rows_all, heads * LANES), F32),
            jax.ShapeDtypeStruct((heads, 8, rows_all), F32),
        ),
        in_specs=[smem, smem] + [vmem] * (CHUNKS + 2),
        out_specs=(vmem,) * 6,
        scratch_shapes=[
            pltpu.VMEM((LANES, rows_all), BF16),
            pltpu.VMEM((heads, rows_all, TILE), F32),
        ],
        compiler_params=pltpu.CompilerParams(vmem_limit_bytes=48 << 20),
        cost_estimate=pl.CostEstimate(
            flops=4 * pairs * LANES, transcendentals=pairs, bytes_accessed=rows_all * 8192
        ),
        name="attend",
    )(table, length, *raws, cos_t, sin_t)


def attend_back_kernel(heads, table, length_ref, query_s, key_s, value_s, ctx_s, lse_s, *refs):
    backs, rest = refs[: 2 * CHUNKS], refs[2 * CHUNKS :]
    cos_t, sin_t, out, back_s, delta_s, key_t, query_acc, key_all, value_all = rest
    rows_all = key_s.shape[0]
    piece = backs[0].shape[0] // BLK
    length = length_ref[0]
    tiles = rows_all // TILE

    for k, back_low in enumerate(backs):

        @pl.loop(0, piece)
        def _(b, k=k, back_low=back_low):
            src = pl.ds(pl.multiple_of(b * BLK, BLK), BLK)
            dst = pl.ds(pl.multiple_of(table[k * piece + b] * BLK, BLK), BLK)
            for h in range(heads):
                cols = slice(h * LANES, (h + 1) * LANES)
                part = back_low[src, cols]
                back_s[h, dst, :] = part
                inner = jnp.sum(part.astype(F32) * ctx_s[dst, cols], axis=1, keepdims=True)
                delta_s[h, :, dst] = jnp.broadcast_to(inner, (BLK, BLK)).T[:8, :]

    @pl.loop(0, rows_all // BLK)
    def _(b):
        rows = pl.ds(pl.multiple_of(b * BLK, BLK), BLK)
        key_t[:, rows] = key_s[rows, :].astype(F32).T.astype(BF16)

    query_acc[...] = jnp.zeros_like(query_acc)
    key_all[...] = jnp.zeros_like(key_all)
    value_all[...] = jnp.zeros_like(value_all)

    def step(i, j, masked):
        k_rows = pl.ds(pl.multiple_of(j * TILE, TILE), TILE)
        q_rows = pl.ds(pl.multiple_of(i * TILE, TILE), TILE)
        key = key_s[k_rows, :]
        value = value_s[k_rows, :]
        value_sum = key_sum = None
        for h in range(heads):
            query = query_s[h, q_rows, :]
            back = back_s[h, q_rows, :]
            tile = dot_t(key, query)
            if masked:
                tile = mask_tile(tile, j * TILE, i * TILE, length)
            soft = jnp.exp(tile * SCALE - lse_s[h, :1, q_rows])
            back_soft = dot_t(value, back)
            low = (soft * (back_soft - delta_s[h, :1, q_rows])).astype(BF16)
            value_part = dot(soft.astype(BF16), back)
            key_part = dot(low, query)
            value_sum = value_part if h == 0 else value_sum + value_part
            key_sum = key_part if h == 0 else key_sum + key_part
            query_acc[h, :, q_rows] += dot(key_t[:, k_rows], low)
        value_all[k_rows, :] += value_sum
        key_all[k_rows, :] += key_sum

    @pl.loop(0, tiles)
    def _(i):
        full = jnp.minimum(i, length // TILE)

        @pl.loop(0, full)
        def _(j):
            step(i, j, False)

        @pl.loop(full, i + 1)
        def _(j):
            step(i, j, True)

    @pl.loop(0, rows_all // BLK)
    def _(b):
        dst = pl.ds(pl.multiple_of(b * BLK, BLK), BLK)
        src = pl.ds(pl.multiple_of(table[b] * BLK, BLK), BLK)
        cos_rows = cos_t[dst, :]
        sin_rows = -sin_t[dst, :]
        for h in range(heads):
            part = query_acc[h, :, src].T * SCALE
            out[dst, h * LANES : (h + 1) * LANES] = turn(part, cos_rows, sin_rows).astype(BF16)
        part = key_all[src, :] * SCALE
        out[dst, heads * LANES : (heads + 1) * LANES] = turn(part, cos_rows, sin_rows).astype(BF16)
        out[dst, (heads + 1) * LANES : (heads + 2) * LANES] = value_all[src, :].astype(BF16)


def attend_back(table, length, saved, backs, cos_t, sin_t, heads):
    query_s, key_s, value_s, ctx_s, lse_s = saved
    rows_all = key_s.shape[0]
    smem = pl.BlockSpec(memory_space=pltpu.SMEM)
    vmem = pl.BlockSpec(memory_space=pltpu.VMEM)
    pairs = heads * rows_all * rows_all // 2
    return pl.pallas_call(
        functools.partial(attend_back_kernel, heads),
        out_shape=jax.ShapeDtypeStruct((rows_all, (heads + 2) * LANES), BF16),
        in_specs=[smem, smem] + [vmem] * (7 + 2 * CHUNKS),
        out_specs=vmem,
        scratch_shapes=[
            pltpu.VMEM((heads, rows_all, LANES), BF16),
            pltpu.VMEM((heads, 8, rows_all), F32),
            pltpu.VMEM((LANES, rows_all), BF16),
            pltpu.VMEM((heads, LANES, rows_all), F32),
            pltpu.VMEM((rows_all, LANES), F32),
            pltpu.VMEM((rows_all, LANES), F32),
        ],
        compiler_params=pltpu.CompilerParams(vmem_limit_bytes=48 << 20),
        cost_estimate=pl.CostEstimate(
            flops=10 * pairs * LANES, transcendentals=pairs, bytes_accessed=rows_all * 8192
        ),
        name="attend_back",
    )(table, length, query_s, key_s, value_s, ctx_s, lse_s, *backs, cos_t, sin_t)


def whole_call(kernel, out_shape, args, name, flops, nbytes):
    vmem = pl.BlockSpec(memory_space=pltpu.VMEM)
    return pl.pallas_call(
        kernel,
        out_shape=out_shape,
        in_specs=[vmem] * len(args),
        out_specs=jax.tree.map(lambda _: vmem, out_shape),
        compiler_params=pltpu.CompilerParams(vmem_limit_bytes=48 << 20),
        cost_estimate=pl.CostEstimate(flops=flops, transcendentals=0, bytes_accessed=nbytes),
        name=name,
    )(*args)


def like(rows, cols, dtype):
    return jax.ShapeDtypeStruct((rows, cols), dtype)


def scale_of(rows):
    return lax.rsqrt(jnp.mean(rows * rows, axis=-1, keepdims=True) + EPS)


def project_kernel(even, odd, weight, gain, low_even, low_odd, raw):
    for source, low, start in ((even, low_even, 0), (odd, low_odd, even.shape[0])):
        for b in range(source.shape[0] // TILE):
            src = slice(b * TILE, (b + 1) * TILE)
            rows_f = source[src, :].astype(F32)
            low[src, :] = (rows_f * scale_of(rows_f) * gain[...]).astype(BF16)
            raw[start + b * TILE : start + (b + 1) * TILE, :] = dot(low[src, :], weight[...])


def project_pair(pair, weight, gain):
    rows = pair[0].shape[0]
    cols = weight.shape[1]
    out = (like(rows, D, BF16), like(rows, D, BF16), like(2 * rows, cols, F32))
    return whole_call(
        project_kernel, out, (*pair, weight, gain), "project", 4 * rows * D * cols, 8 * rows * D
    )


def project_back_kernel(turned, weight, even, odd, sum_even, sum_odd, gain_sum):
    total = jnp.zeros((1, D), F32)
    for tokens, out, start in ((odd, sum_odd, even.shape[0]), (even, sum_even, 0)):
        for b in range(tokens.shape[0] // TILE):
            dst = slice(b * TILE, (b + 1) * TILE)
            rows_f = tokens[dst, :].astype(F32)
            part = dot_t(turned[start + b * TILE : start + (b + 1) * TILE, :], weight[...])
            out[dst, :] = part.astype(out.dtype)
            total = total + jnp.sum(part * rows_f * scale_of(rows_f), axis=0, keepdims=True)
    gain_sum[...] = jnp.broadcast_to(total, gain_sum.shape)


def project_back_pair(turned, weight, pair):
    rows = pair[0].shape[0]
    cols = weight.shape[1]
    out = (like(rows, D, F32), like(rows, D, BF16), like(8, D, F32))
    return whole_call(
        project_back_kernel, out, (turned, weight, *pair), "project_back",
        4 * rows * D * cols, 10 * rows * D,
    )


def feed_kernel(
    feed_even, feed_odd, cot_even, cot_odd, live, pair_w, down_w, low_even, low_odd, hidden,
    pair_back, sum_even, sum_odd,
):
    units = down_w.shape[0]
    halves = (
        (feed_odd, cot_odd, low_odd, sum_odd, feed_even.shape[0]),
        (feed_even, cot_even, low_even, sum_even, 0),
    )
    for feed, cot, low, out, start in halves:
        for b in range(feed.shape[0] // TILE):
            here = slice(b * TILE, (b + 1) * TILE)
            both = slice(start + b * TILE, start + (b + 1) * TILE)
            low[here, :] = (cot[here, :].astype(F32) * live[both, :]).astype(BF16)
            gate_pre = dot(feed[here, :], pair_w[:, :units])
            up_pre = dot(feed[here, :], pair_w[:, units:])
            back_hidden = dot_t(low[here, :], down_w[...])
            gate_sigmoid = jax.nn.sigmoid(gate_pre)
            gate_silu = gate_pre * gate_sigmoid
            hidden[both, :] = (gate_silu * up_pre).astype(BF16)
            pair_back[both, :units] = (
                back_hidden * up_pre * gate_sigmoid * (1.0 + gate_pre * (1.0 - gate_sigmoid))
            ).astype(BF16)
            pair_back[both, units:] = (back_hidden * gate_silu).astype(BF16)
            out[here, :] = dot_t(pair_back[both, :], pair_w[...]).astype(out.dtype)


def feed_pair(feed, cot, live, pair_w, down_w):
    rows = feed[0].shape[0]
    units = down_w.shape[0]
    out = (
        like(rows, D, BF16), like(rows, D, BF16), like(2 * rows, units, BF16),
        like(2 * rows, 2 * units, BF16), like(rows, D, F32), like(rows, D, BF16),
    )
    return whole_call(
        feed_kernel, out, (*feed, *cot, live, pair_w, down_w), "feed",
        20 * rows * D * units, 20 * rows * D,
    )


def cut_kernel(me, gate, up, out):
    @pl.when(pl.program_id(0) == 0)
    def _():
        out[...] = gate[...]

    @pl.when(pl.program_id(0) == 1)
    def _():
        out[...] = up[...]


def cut_columns(me, gate, up, planes, size):
    shard, ff = gate.shape
    mine = ff // planes // size
    if mine % LANES:
        cut = [
            lax.dynamic_slice_in_dim(w.reshape(shard, planes, size, mine), me, 1, 2)
            for w in (gate, up)
        ]
        return jnp.concatenate([c.reshape(shard, planes * mine) for c in cut], axis=1)
    block = pl.BlockSpec((shard, mine), lambda g, z, me_ref: (0, z * size + me_ref[0]))
    return pl.pallas_call(
        cut_kernel,
        out_shape=like(shard, 2 * planes * mine, BF16),
        grid_spec=pltpu.PrefetchScalarGridSpec(
            num_scalar_prefetch=1,
            grid=(2, planes),
            in_specs=[block, block],
            out_specs=pl.BlockSpec((shard, mine), lambda g, z, me_ref: (0, g * planes + z)),
        ),
        name="cut",
    )(me.reshape(1).astype(jnp.int32), gate, up)


def spread_kernel(order, *refs):
    size = (len(refs) - 2) // 2
    gate, up = refs[-2:]
    for r in range(size):
        cols = pl.ds(pl.multiple_of(order[r] * LANES, LANES), LANES)
        gate[:, cols] = refs[r][...].astype(F32)
        up[:, cols] = refs[size + r][...].astype(F32)


def spread_columns(block, planes, size, order):
    shard, both = block.shape
    mine = both // 2 // planes
    ff = both // 2 * size
    if size != 8 or mine != LANES:
        pieces = lax.all_gather(block, "ctx", axis=0)
        wide = pieces.reshape(size, shard, 2, planes, mine).transpose(2, 1, 3, 0, 4)
        wide = wide.reshape(2, shard, ff).astype(F32)
        return wide[0], wide[1]
    pieces = [part for pair in gather_rows(block, size) for part in pair]
    out = pl.BlockSpec((shard, size * mine), lambda z, order_ref: (0, z))
    gate_in = pl.BlockSpec((shard, mine), lambda z, order_ref: (0, z))
    up_in = pl.BlockSpec((shard, mine), lambda z, order_ref: (0, planes + z))
    return pl.pallas_call(
        spread_kernel,
        out_shape=(like(shard, ff, F32), like(shard, ff, F32)),
        grid_spec=pltpu.PrefetchScalarGridSpec(
            num_scalar_prefetch=1,
            grid=(planes,),
            in_specs=[gate_in] * size + [up_in] * size,
            out_specs=(out, out),
        ),
        name="spread",
    )(order, *pieces, *pieces)


def compact_matrix(rows, cols, place):
    source = lax.broadcasted_iota(jnp.int32, (rows, cols), 0)
    target = lax.broadcasted_iota(jnp.int32, (rows, cols), 1)
    return (source == place(target)).astype(BF16)


def heads_kernel(heads, shares, pieces, query, key, value, out):
    size = pieces.shape[0]
    shard = query.shape[0]
    group = LANES * 3

    def select(parts):
        width = pieces.shape[2]
        source = lax.broadcasted_iota(jnp.int32, (width, group), 0)
        target = lax.broadcasted_iota(jnp.int32, (width, group), 1)
        total = None
        for slot, (device, start, span) in enumerate(parts):
            inside = (target >= slot * span) & (target < (slot + 1) * span)
            choose = (inside & (source == target - slot * span + start)).astype(BF16)
            part = dot(pieces[device, :shard, :], choose)
            total = part if total is None else total + part
        return total

    q_cols = heads * HEAD_WIDTH
    per = group // q_cols
    for j in range(size // per):
        parts = [(j * per + i, 0, q_cols) for i in range(per)]
        query[:, j * group : (j + 1) * group] = select(parts)
    per = group // HEAD_WIDTH
    for target, start in ((key, q_cols), (value, q_cols + HEAD_WIDTH)):
        for j in range(KEY_VALUE_HEADS // per):
            parts = [((j * per + i) * shares, start, HEAD_WIDTH) for i in range(per)]
            target[:, j * group : (j + 1) * group] = select(parts)
    rows = pieces.shape[1] - shard
    for z in range(size // 2):
        for q in range(2):
            out[q * rows : (q + 1) * rows, z * shard : (z + 1) * shard] = pieces[
                2 * z + q, shard:, :shard
            ].astype(F32)


def spread_heads(pieces, heads, shares, shard):
    kv = KEY_VALUE_HEADS * HEAD_WIDTH
    out = (like(shard, D, F32), like(shard, kv, F32), like(shard, kv, F32), like(shard, D, F32))
    return whole_call(
        functools.partial(heads_kernel, heads, shares), out, (pieces,), "heads",
        4 * shard * D * D, 8 * shard * D,
    )


def after(value, *others):
    return lax.optimization_barrier((value, *others))[0]


def hop(value, size, bit):
    return lax.ppermute(value, "ctx", [(i, i ^ bit) for i in range(size)])


def gather_rows(block, size):
    if size != 8:
        whole = lax.all_gather(block, "ctx", axis=0, tiled=True)
        return [tuple(jnp.split(part, 2)) for part in jnp.split(whole, CHUNKS)]
    half = block.shape[0] // 2
    across = hop(block, size, 2)
    along = hop(block, size, 4)
    upper = hop(along[:half], size, 2)
    lower = hop(across[half:], size, 4)
    corner = jnp.concatenate([upper, lower])
    return [(part, hop(part, size, 1)) for part in (block, across, along, corner)]


def scatter_rows(pairs, size, before_last=()):
    if size != 8:
        whole = jnp.concatenate([part.astype(BF16) for pair in pairs for part in pair])
        total = lax.psum_scatter(whole, "ctx", scatter_dimension=0, tiled=True).astype(F32)
        return total, total

    def fold(k):
        even, odd = pairs[k]
        return even + hop(odd.astype(BF16), size, 1).astype(F32)

    corner, across, along, own = fold(3), fold(1), fold(2), fold(0)
    half = own.shape[0] // 2

    def send(value, bit):
        return hop(value.astype(BF16), size, bit).astype(F32)

    for_along = send(corner[:half], 2)
    for_across = send(corner[half:], 4)
    across_top = send(across[:half], 2)
    along_low = send(along[half:], 4)
    across_rest = (across[half:] + for_across).astype(BF16)
    along_rest = (along[:half] + for_along).astype(BF16)
    if before_last:
        across_rest, along_rest, *_ = lax.optimization_barrier(
            (across_rest, along_rest, *before_last)
        )
    across_low = send(across_rest, 2)
    along_top = send(along_rest, 4)
    total = jnp.concatenate(
        [own[:half] + across_top + along_top, own[half:] + across_low + along_low]
    )
    return total, along_rest


def swap_planes(value, size, planes):
    moves = []
    for chip in range(size // 2):
        for core in range(2):
            for z in range(planes):
                moves.append(((chip * 2 + core) * planes + z, (z * 2 + core) * planes + chip))
    return lax.ppermute(value, ("ctx", "fsdp"), moves)


def norm_back(residual, scale_rows, gain, upstream):
    weighted = upstream * gain
    row_inner = jnp.mean(weighted * residual, axis=-1, keepdims=True)
    return scale_rows * weighted - residual * (scale_rows * scale_rows * scale_rows) * row_inner


def pad_turned(weight):
    rows, cols = weight.shape
    split = weight.reshape(rows, cols // HALF, HALF)
    return jnp.pad(split, ((0, 0), (0, 0), (0, LANES // 2 - HALF))).reshape(rows, -1)


def local(
    size,
    planes,
    tokens,
    cotangent,
    attend_gain,
    w_query,
    w_key,
    w_value,
    w_out,
    feed_gain,
    w_gate,
    w_up,
    w_down,
    lengths,
    deal_table,
):
    me = lax.axis_index("ctx")
    plane = lax.axis_index("fsdp")
    rows_here = tokens.shape[1]
    rows_all = rows_here * size
    heads = QUERY_HEADS // size
    shares = max(1, size // KEY_VALUE_HEADS)
    shard = w_query.shape[0]
    ff = w_gate.shape[1]
    ff_mine = ff // planes // size
    q_cols = heads * HEAD_WIDTH
    key_head = me // shares
    turn_cols = (heads + 1) * LANES
    piece = rows_all // CHUNKS

    turn_mine = q_cols + HEAD_WIDTH
    cut_cols = turn_mine + HEAD_WIDTH
    wide_cols = turn_cols + LANES

    def place(target):
        turned_col = (target // HALF) * (LANES // 2) + lax.rem(target, HALF)
        return jnp.where(target < turn_mine, turned_col, target - turn_mine + turn_cols)

    compact = compact_matrix(wide_cols, cut_cols, place)
    with jax.named_scope("weights_proj"):
        query_cut = lax.dynamic_slice_in_dim(w_query, me * q_cols, q_cols, 1)
        key_cut = lax.dynamic_slice_in_dim(w_key, key_head * HEAD_WIDTH, HEAD_WIDTH, 1)
        value_cut = lax.dynamic_slice_in_dim(w_value, key_head * HEAD_WIDTH, HEAD_WIDTH, 1)
        gains = jnp.stack([attend_gain, feed_gain])
        gains = jnp.pad(gains, ((0, 14), (0, cut_cols - shard)))
        proj_cut = jnp.concatenate([query_cut, key_cut, value_cut], axis=1)
        proj_all = lax.all_gather(jnp.concatenate([proj_cut, gains]), "fsdp", axis=0)
        gain_one = proj_all[:, shard, :shard].reshape(1, D).astype(F32)
        gain_two = proj_all[:, shard + 1, :shard].reshape(1, D).astype(F32)
        proj_w = dot_t(proj_all[:, :shard].reshape(D, cut_cols), compact).astype(BF16)
    with jax.named_scope("weights_out"):
        out_piece = lax.dynamic_slice(
            w_out, (lax.rem(me, 2) * q_cols, (me // 2) * shard), (q_cols, shard)
        )
        out_piece = swap_planes(out_piece, size, planes)
        out_w = lax.all_gather(out_piece, "fsdp", axis=0)
        out_w = out_w.transpose(1, 0, 2).reshape(heads, HEAD_WIDTH, D)
        out_w = jnp.pad(out_w, ((0, 0), (0, LANES - HEAD_WIDTH), (0, 0)))
        out_w = out_w.reshape(heads * LANES, D)
    with jax.named_scope("weights_pair"):
        pair_w = lax.all_gather(
            cut_columns(me, w_gate, w_up, planes, size), "fsdp", axis=0, tiled=True
        )
    with jax.named_scope("weights_down"):
        down_w = lax.all_gather(
            lax.dynamic_slice_in_dim(w_down, me * ff_mine, ff_mine, 0), "fsdp", axis=0, tiled=True
        )

    order = jnp.arange(size, dtype=jnp.int32)
    if size == 8:
        order = jnp.bitwise_xor(order, me)
    table = deal_table.reshape(size, rows_here // BLK)[order].reshape(-1)
    pos_all = (table[:, None] * BLK + jnp.arange(BLK, dtype=jnp.int32)[None, :]).reshape(-1)
    live_all = (pos_all < lengths[0]).astype(F32)[:, None]
    if size == 8:
        live = live_all[:rows_here]
    else:
        live = lax.dynamic_slice_in_dim(live_all, me * rows_here, rows_here)
    frequency = ROPE_BASE ** (-2.0 * jnp.arange(HALF, dtype=F32) / HEAD_WIDTH)
    angles = pos_all.astype(F32)[:, None] * frequency[None, :]
    pad = jnp.zeros((rows_all, LANES // 2 - HALF), F32)
    cosine, sine = jnp.cos(angles), jnp.sin(angles)
    cos_t = jnp.concatenate([cosine, pad, cosine, pad], axis=1)
    sin_t = jnp.concatenate([-sine, pad, sine, pad], axis=1)

    def part_of(array, k):
        return array[k * piece : (k + 1) * piece]

    def project_rows(rows, weight):
        half = rows.shape[0] // 2
        odd = dot(rows[half:], weight).astype(BF16)
        return dot(rows[:half], weight), odd

    with jax.named_scope("tokens"):
        token_pairs = gather_rows(tokens[0], size)
    residual = tokens[0].astype(F32)
    scale_one = scale_of(residual)
    attend_low, raws = [], []
    for pair in token_pairs:
        even, odd, raw = project_pair(pair, proj_w, gain_one)
        attend_low += [even, odd]
        raws.append(raw)
    ctx_low, *saved = attend(table, lengths, raws, cos_t, sin_t, heads)
    with jax.named_scope("branch"):
        attend_branch, _ = scatter_rows(
            [project_rows(part_of(ctx_low, k), out_w) for k in range(CHUNKS)], size
        )
    middle = residual + attend_branch

    with jax.named_scope("cotangent"):
        cot_pairs = gather_rows(after(cotangent[0], token_pairs[3][0]), size)
    scale_two = scale_of(middle)
    with jax.named_scope("feed_in"):
        feed_pairs = gather_rows((middle * scale_two * gain_two).astype(BF16), size)
    back_low, hidden, pair_back, sums_in = [], [], [], []
    for k in range(CHUNKS):
        low_even, low_odd, hidden_k, pair_k, sum_even, sum_odd = feed_pair(
            feed_pairs[k], cot_pairs[k], part_of(live_all, k), pair_w, down_w
        )
        back_low += [low_even, low_odd]
        hidden.append(hidden_k)
        pair_back.append(pair_k)
        sums_in.append((sum_even, sum_odd))
    with jax.named_scope("grad_pair"):
        feed_all = jnp.concatenate([block for pair in feed_pairs for block in pair])
        pair_grad = dot_outer(feed_all, jnp.concatenate(pair_back)).astype(BF16)
    with jax.named_scope("grad_down"):
        down_grad = dot_outer(jnp.concatenate(hidden), jnp.concatenate(back_low)).astype(BF16)
    with jax.named_scope("back_feed"):
        back_feed_in, _ = scatter_rows(sums_in, size, (pair_grad, down_grad))
    with jax.named_scope("grad_pair"):
        pair_grad = lax.psum_scatter(pair_grad, "fsdp", scatter_dimension=0, tiled=True)
    with jax.named_scope("grad_down"):
        down_grad = lax.psum_scatter(down_grad, "fsdp", scatter_dimension=0, tiled=True)
    back_final = cotangent[0].astype(F32) * live
    back_middle = back_final + norm_back(middle, scale_two, gain_two, back_feed_in)
    gain_two_grad = jnp.sum(back_feed_in * middle * scale_two, axis=0)

    with jax.named_scope("back_mid"):
        mid_pairs = gather_rows(back_middle.astype(BF16), size)
    mid_blocks = [block for pair in mid_pairs for block in pair]
    with jax.named_scope("grad_down"):
        grad_down = lax.all_gather(
            after(down_grad, mid_blocks[-1]), "ctx", axis=0, tiled=True
        ).astype(F32)
    with jax.named_scope("grad_pair"):
        grad_gate, grad_up = spread_columns(
            after(pair_grad, mid_blocks[-1]), planes, size, order
        )
    back_context = [dot_t(block, out_w).astype(BF16) for block in mid_blocks]
    turned = attend_back(table, lengths, saved, back_context, cos_t, sin_t, heads)
    if shares > 1:
        pairs = [[g * shares + i for i in range(shares)] for g in range(size // shares)]
        both = lax.psum(turned[:, heads * LANES :].astype(F32), "ctx", axis_index_groups=pairs)
        first = (lax.rem(me, shares) == 0).astype(F32)
        turned = jnp.concatenate([turned[:, : heads * LANES], (both * first).astype(BF16)], axis=1)
    sums_in, gain_sums = [], []
    for k in range(CHUNKS):
        sum_even, sum_odd, gain_sum = project_back_pair(
            part_of(turned, k), proj_w, token_pairs[k]
        )
        sums_in.append((sum_even, sum_odd))
        gain_sums.append(gain_sum)
    with jax.named_scope("back_attend"):
        back_attend_in, attend_sent = scatter_rows(sums_in, size)
    grad_tokens = back_middle + norm_back(residual, scale_one, gain_one, back_attend_in)
    gain_one_grad = (gain_sums[0] + gain_sums[1] + gain_sums[2] + gain_sums[3])[0]

    with jax.named_scope("grad_heads"):
        narrow = dot(turned, compact).astype(BF16)
        proj_grad = dot_outer(jnp.concatenate(attend_low), narrow).astype(BF16)
        out_grad = dot_outer(ctx_low, jnp.concatenate(mid_blocks)).astype(BF16)
        out_grad = out_grad.reshape(heads, LANES, planes, shard)[:, :HEAD_WIDTH]
        out_grad = out_grad.reshape(q_cols, planes, shard).transpose(1, 0, 2)
        out_grad = jnp.pad(out_grad, ((0, 0), (0, 0), (0, cut_cols - shard)))
        head_grad = jnp.concatenate([proj_grad.reshape(planes, shard, cut_cols), out_grad], axis=1)
        head_grad = lax.psum_scatter(head_grad, "fsdp", scatter_dimension=0, tiled=True)[0]
        out_piece = swap_planes(head_grad[shard:], size, planes)
        head_grad = lax.all_gather(
            jnp.concatenate([head_grad[:shard], out_piece]), "ctx", axis=0
        )
        grad_query, grad_key, grad_value, grad_out = spread_heads(head_grad, heads, shares, shard)

    with jax.named_scope("feed_branch"):
        parts = [project_rows(after(h, back_middle), down_w) for h in hidden]
        parts = [(even, after(odd, mid_blocks[-1])) for even, odd in parts]
        feed_branch, _ = scatter_rows(parts, size)
    final_sum = middle + feed_branch
    layer_out = (final_sum * live).astype(BF16)
    sums = jnp.stack(
        [
            jnp.sum(final_sum * final_sum * live),
            jnp.sum(attend_branch * attend_branch * live),
            jnp.sum(feed_branch * feed_branch * live),
        ]
    )

    with jax.named_scope("small"):
        slot = (jnp.arange(planes) == plane).astype(F32)
        stats = jnp.pad(slot[:, None] * sums[None, :], ((0, 0), (0, LANES - 3))).reshape(-1)
        small = lax.psum(
            after(jnp.concatenate([gain_one_grad, gain_two_grad, stats]), attend_sent),
            ("ctx", "fsdp"),
        )
    grad_attend_gain = lax.dynamic_slice_in_dim(small[:D], plane * shard, shard)
    grad_feed_gain = lax.dynamic_slice_in_dim(small[D : 2 * D], plane * shard, shard)
    total_sums = lax.dynamic_slice_in_dim(small[2 * D :].reshape(planes, LANES), plane, 1)[:, :3]
    rms_stats = jnp.sqrt(total_sums / (lengths.astype(F32)[:, None] * D))
    return (
        layer_out[None],
        grad_tokens[None],
        grad_attend_gain,
        grad_query,
        grad_key,
        grad_value,
        grad_out,
        grad_feed_gain,
        grad_gate,
        grad_up,
        grad_down,
        rms_stats,
    )


def solution(mesh):
    rows = P("fsdp", "ctx", None)
    vector = P("fsdp")
    matrix = P("fsdp", None)
    in_specs = (rows, rows, vector, matrix, matrix, matrix, matrix, vector, matrix, matrix, matrix)
    in_specs += (vector, P())
    out_specs = (rows, rows, vector, matrix, matrix, matrix, matrix, vector, matrix, matrix, matrix)
    out_specs += (matrix,)
    body = functools.partial(local, mesh.shape["ctx"], mesh.shape["fsdp"])
    return jax.shard_map(
        body, mesh=mesh, in_specs=in_specs, out_specs=out_specs, check_vma=False
    )
```

```python
import functools
import math

import jax
import jax.numpy as jnp
from jax import lax
from jax.experimental import pallas as pl
from jax.experimental.pallas import tpu as pltpu
from jax.sharding import PartitionSpec as P


D = 1536
QUERY_HEADS = 16
KEY_VALUE_HEADS = 8
HEAD_WIDTH = 96
HALF = HEAD_WIDTH // 2
BLK = 128
LANES = 128

EPS = 1e-05
ROPE_BASE = 10000.0
NEG = -1e30
SCALE = 1.0 / math.sqrt(HEAD_WIDTH)
TILE = 256
CHUNKS = 4

F32 = jnp.float32
BF16 = jnp.bfloat16


def dot(left, right):
    return lax.dot_general(left, right, (((1,), (0,)), ((), ())), preferred_element_type=F32)


def dot_t(left, right):
    return lax.dot_general(left, right, (((1,), (1,)), ((), ())), preferred_element_type=F32)


def dot_outer(left, right):
    return lax.dot_general(left, right, (((0,), (0,)), ((), ())), preferred_element_type=F32)


def turn(rows, cos_rows, sin_rows):
    return rows * cos_rows + pltpu.roll(rows, LANES // 2, 1) * sin_rows


def mask_tile(scores, key_start, query_start, length):
    key_pos = key_start + lax.broadcasted_iota(jnp.int32, scores.shape, 0)
    query_pos = query_start + lax.broadcasted_iota(jnp.int32, scores.shape, 1)
    return jnp.where((key_pos <= query_pos) & (key_pos < length), scores, NEG)


def attend_kernel(heads, table, length_ref, *refs):
    raws, rest = refs[:CHUNKS], refs[CHUNKS:]
    cos_t, sin_t, ctx_low, query_s, key_s, value_s, ctx_s, lse_s, value_t, score_s = rest
    rows_all = key_s.shape[0]
    piece = raws[0].shape[0] // BLK
    length = length_ref[0]

    for k, raw in enumerate(raws):

        @pl.loop(0, piece)
        def _(b, k=k, raw=raw):
            src = pl.ds(pl.multiple_of(b * BLK, BLK), BLK)
            here = pl.ds(pl.multiple_of((k * piece + b) * BLK, BLK), BLK)
            dst = pl.ds(pl.multiple_of(table[k * piece + b] * BLK, BLK), BLK)
            cos_rows = cos_t[here, :]
            sin_rows = sin_t[here, :]
            for h in range(heads):
                part = raw[src, h * LANES : (h + 1) * LANES]
                query_s[h, dst, :] = turn(part, cos_rows, sin_rows).astype(BF16)
            part = raw[src, heads * LANES : (heads + 1) * LANES]
            key_s[dst, :] = turn(part, cos_rows, sin_rows).astype(BF16)
            part = raw[src, (heads + 1) * LANES : (heads + 2) * LANES]
            value_s[dst, :] = part.astype(BF16)
            value_t[:, dst] = part.T.astype(BF16)

    every = range(heads)

    @pl.loop(0, rows_all // TILE)
    def _(i):
        q_rows = pl.ds(pl.multiple_of(i * TILE, TILE), TILE)
        full = jnp.minimum(i, length // TILE)

        def score(j, tops, masked):
            k_rows = pl.ds(pl.multiple_of(j * TILE, TILE), TILE)
            key = key_s[k_rows, :]
            out = []
            for h in every:
                tile = dot_t(key, query_s[h, q_rows, :])
                if masked:
                    tile = mask_tile(tile, j * TILE, i * TILE, length)
                score_s[h, k_rows, :] = tile
                out.append(jnp.maximum(tops[h], jnp.max(tile, axis=0, keepdims=True)))
            return tuple(out)

        tops = tuple(jnp.full((1, TILE), NEG, F32) for _ in every)
        tops = lax.fori_loop(0, full, lambda j, t: score(j, t, False), tops)
        tops = lax.fori_loop(full, i + 1, lambda j, t: score(j, t, True), tops)

        def accumulate(j, carry):
            k_rows = pl.ds(pl.multiple_of(j * TILE, TILE), TILE)
            out = []
            for h in every:
                total, context = carry[h]
                weight = jnp.exp((score_s[h, k_rows, :] - tops[h]) * SCALE)
                total = total + jnp.sum(weight, axis=0, keepdims=True)
                context = context + dot(value_t[:, k_rows], weight.astype(BF16))
                out.append((total, context))
            return tuple(out)

        start = tuple((jnp.zeros((1, TILE), F32), jnp.zeros((LANES, TILE), F32)) for _ in every)
        sums = lax.fori_loop(0, i + 1, accumulate, start)
        for h in every:
            total, context = sums[h]
            ctx_s[q_rows, h * LANES : (h + 1) * LANES] = (context / total).T
            lse_s[h, :, q_rows] = jnp.broadcast_to(tops[h] * SCALE + jnp.log(total), (8, TILE))

    @pl.loop(0, rows_all // BLK)
    def _(b):
        dst = pl.ds(pl.multiple_of(b * BLK, BLK), BLK)
        src = pl.ds(pl.multiple_of(table[b] * BLK, BLK), BLK)
        ctx_low[dst, :] = ctx_s[src, :].astype(BF16)


def attend(table, length, raws, cos_t, sin_t, heads):
    rows_all = cos_t.shape[0]
    smem = pl.BlockSpec(memory_space=pltpu.SMEM)
    vmem = pl.BlockSpec(memory_space=pltpu.VMEM)
    pairs = heads * rows_all * rows_all // 2
    return pl.pallas_call(
        functools.partial(attend_kernel, heads),
        out_shape=(
            jax.ShapeDtypeStruct((rows_all, heads * LANES), BF16),
            jax.ShapeDtypeStruct((heads, rows_all, LANES), BF16),
            jax.ShapeDtypeStruct((rows_all, LANES), BF16),
            jax.ShapeDtypeStruct((rows_all, LANES), BF16),
            jax.ShapeDtypeStruct((rows_all, heads * LANES), F32),
            jax.ShapeDtypeStruct((heads, 8, rows_all), F32),
        ),
        in_specs=[smem, smem] + [vmem] * (CHUNKS + 2),
        out_specs=(vmem,) * 6,
        scratch_shapes=[
            pltpu.VMEM((LANES, rows_all), BF16),
            pltpu.VMEM((heads, rows_all, TILE), F32),
        ],
        compiler_params=pltpu.CompilerParams(vmem_limit_bytes=48 << 20),
        cost_estimate=pl.CostEstimate(
            flops=4 * pairs * LANES, transcendentals=pairs, bytes_accessed=rows_all * 8192
        ),
        name="attend",
    )(table, length, *raws, cos_t, sin_t)


def attend_back_kernel(heads, table, length_ref, query_s, key_s, value_s, ctx_s, lse_s, *refs):
    backs, rest = refs[: 2 * CHUNKS], refs[2 * CHUNKS :]
    cos_t, sin_t, out, back_s, delta_s, key_t, query_acc, key_all, value_all = rest
    rows_all = key_s.shape[0]
    piece = backs[0].shape[0] // BLK
    length = length_ref[0]
    tiles = rows_all // TILE

    for k, back_low in enumerate(backs):

        @pl.loop(0, piece)
        def _(b, k=k, back_low=back_low):
            src = pl.ds(pl.multiple_of(b * BLK, BLK), BLK)
            dst = pl.ds(pl.multiple_of(table[k * piece + b] * BLK, BLK), BLK)
            for h in range(heads):
                cols = slice(h * LANES, (h + 1) * LANES)
                part = back_low[src, cols]
                back_s[h, dst, :] = part
                inner = jnp.sum(part.astype(F32) * ctx_s[dst, cols], axis=1, keepdims=True)
                delta_s[h, :, dst] = jnp.broadcast_to(inner, (BLK, BLK)).T[:8, :]

    @pl.loop(0, rows_all // BLK)
    def _(b):
        rows = pl.ds(pl.multiple_of(b * BLK, BLK), BLK)
        key_t[:, rows] = key_s[rows, :].astype(F32).T.astype(BF16)

    query_acc[...] = jnp.zeros_like(query_acc)
    key_all[...] = jnp.zeros_like(key_all)
    value_all[...] = jnp.zeros_like(value_all)

    def step(i, j, masked):
        k_rows = pl.ds(pl.multiple_of(j * TILE, TILE), TILE)
        q_rows = pl.ds(pl.multiple_of(i * TILE, TILE), TILE)
        key = key_s[k_rows, :]
        value = value_s[k_rows, :]
        value_sum = key_sum = None
        for h in range(heads):
            query = query_s[h, q_rows, :]
            back = back_s[h, q_rows, :]
            tile = dot_t(key, query)
            if masked:
                tile = mask_tile(tile, j * TILE, i * TILE, length)
            soft = jnp.exp(tile * SCALE - lse_s[h, :1, q_rows])
            back_soft = dot_t(value, back)
            low = (soft * (back_soft - delta_s[h, :1, q_rows])).astype(BF16)
            value_part = dot(soft.astype(BF16), back)
            key_part = dot(low, query)
            value_sum = value_part if h == 0 else value_sum + value_part
            key_sum = key_part if h == 0 else key_sum + key_part
            query_acc[h, :, q_rows] += dot(key_t[:, k_rows], low)
        value_all[k_rows, :] += value_sum
        key_all[k_rows, :] += key_sum

    @pl.loop(0, tiles)
    def _(i):
        full = jnp.minimum(i, length // TILE)

        @pl.loop(0, full)
        def _(j):
            step(i, j, False)

        @pl.loop(full, i + 1)
        def _(j):
            step(i, j, True)

    @pl.loop(0, rows_all // BLK)
    def _(b):
        dst = pl.ds(pl.multiple_of(b * BLK, BLK), BLK)
        src = pl.ds(pl.multiple_of(table[b] * BLK, BLK), BLK)
        cos_rows = cos_t[dst, :]
        sin_rows = -sin_t[dst, :]
        for h in range(heads):
            part = query_acc[h, :, src].T * SCALE
            out[dst, h * LANES : (h + 1) * LANES] = turn(part, cos_rows, sin_rows).astype(BF16)
        part = key_all[src, :] * SCALE
        out[dst, heads * LANES : (heads + 1) * LANES] = turn(part, cos_rows, sin_rows).astype(BF16)
        out[dst, (heads + 1) * LANES : (heads + 2) * LANES] = value_all[src, :].astype(BF16)


def attend_back(table, length, saved, backs, cos_t, sin_t, heads):
    query_s, key_s, value_s, ctx_s, lse_s = saved
    rows_all = key_s.shape[0]
    smem = pl.BlockSpec(memory_space=pltpu.SMEM)
    vmem = pl.BlockSpec(memory_space=pltpu.VMEM)
    pairs = heads * rows_all * rows_all // 2
    return pl.pallas_call(
        functools.partial(attend_back_kernel, heads),
        out_shape=jax.ShapeDtypeStruct((rows_all, (heads + 2) * LANES), BF16),
        in_specs=[smem, smem] + [vmem] * (7 + 2 * CHUNKS),
        out_specs=vmem,
        scratch_shapes=[
            pltpu.VMEM((heads, rows_all, LANES), BF16),
            pltpu.VMEM((heads, 8, rows_all), F32),
            pltpu.VMEM((LANES, rows_all), BF16),
            pltpu.VMEM((heads, LANES, rows_all), F32),
            pltpu.VMEM((rows_all, LANES), F32),
            pltpu.VMEM((rows_all, LANES), F32),
        ],
        compiler_params=pltpu.CompilerParams(vmem_limit_bytes=48 << 20),
        cost_estimate=pl.CostEstimate(
            flops=10 * pairs * LANES, transcendentals=pairs, bytes_accessed=rows_all * 8192
        ),
        name="attend_back",
    )(table, length, query_s, key_s, value_s, ctx_s, lse_s, *backs, cos_t, sin_t)


def whole_call(kernel, out_shape, args, flops, nbytes):
    vmem = pl.BlockSpec(memory_space=pltpu.VMEM)
    return pl.pallas_call(
        kernel,
        out_shape=out_shape,
        in_specs=[vmem] * len(args),
        out_specs=jax.tree.map(lambda _: vmem, out_shape),
        compiler_params=pltpu.CompilerParams(vmem_limit_bytes=48 << 20),
        cost_estimate=pl.CostEstimate(flops=flops, transcendentals=0, bytes_accessed=nbytes),
    )(*args)


def like(rows, cols, dtype):
    return jax.ShapeDtypeStruct((rows, cols), dtype)


def scale_of(rows):
    return lax.rsqrt(jnp.mean(rows * rows, axis=-1, keepdims=True) + EPS)


def project_kernel(even, odd, weight, gain, low_even, low_odd, raw):
    for source, low, start in ((even, low_even, 0), (odd, low_odd, even.shape[0])):
        for b in range(source.shape[0] // TILE):
            src = slice(b * TILE, (b + 1) * TILE)
            rows_f = source[src, :].astype(F32)
            low[src, :] = (rows_f * scale_of(rows_f) * gain[...]).astype(BF16)
            raw[start + b * TILE : start + (b + 1) * TILE, :] = dot(low[src, :], weight[...])


def project_pair(pair, weight, gain):
    rows = pair[0].shape[0]
    cols = weight.shape[1]
    out = (like(rows, D, BF16), like(rows, D, BF16), like(2 * rows, cols, F32))
    return whole_call(project_kernel, out, (*pair, weight, gain), 4 * rows * D * cols, 8 * rows * D)


def project_back_kernel(turned, weight, even, odd, sum_even, sum_odd, gain_sum):
    total = jnp.zeros((1, D), F32)
    for tokens, out, start in ((odd, sum_odd, even.shape[0]), (even, sum_even, 0)):
        for b in range(tokens.shape[0] // TILE):
            dst = slice(b * TILE, (b + 1) * TILE)
            rows_f = tokens[dst, :].astype(F32)
            part = dot_t(turned[start + b * TILE : start + (b + 1) * TILE, :], weight[...])
            out[dst, :] = part.astype(out.dtype)
            total = total + jnp.sum(part * rows_f * scale_of(rows_f), axis=0, keepdims=True)
    gain_sum[...] = jnp.broadcast_to(total, gain_sum.shape)


def project_back_pair(turned, weight, pair):
    rows = pair[0].shape[0]
    cols = weight.shape[1]
    out = (like(rows, D, F32), like(rows, D, BF16), like(8, D, F32))
    return whole_call(
        project_back_kernel, out, (turned, weight, *pair),
        4 * rows * D * cols, 10 * rows * D,
    )


def feed_kernel(
    feed_even, feed_odd, cot_even, cot_odd, live, pair_w, down_w, low_even, low_odd, hidden,
    pair_back, sum_even, sum_odd,
):
    units = down_w.shape[0]
    half = TILE
    for b in range(feed_even.shape[0] // half):
        here = slice(b * half, (b + 1) * half)
        other = slice(feed_even.shape[0] + b * half, feed_even.shape[0] + (b + 1) * half)
        low_even[here, :] = (cot_even[here, :].astype(F32) * live[here, :]).astype(BF16)
        low_odd[here, :] = (cot_odd[here, :].astype(F32) * live[other, :]).astype(BF16)
        feed = jnp.concatenate([feed_even[here, :], feed_odd[here, :]])
        low = jnp.concatenate([low_even[here, :], low_odd[here, :]])
        gate_pre = dot(feed, pair_w[:, :units])
        up_pre = dot(feed, pair_w[:, units:])
        back_hidden = dot_t(low, down_w[...])
        gate_sigmoid = jax.nn.sigmoid(gate_pre)
        gate_silu = gate_pre * gate_sigmoid
        act = (gate_silu * up_pre).astype(BF16)
        gate_back = (
            back_hidden * up_pre * gate_sigmoid * (1.0 + gate_pre * (1.0 - gate_sigmoid))
        ).astype(BF16)
        up_back = (back_hidden * gate_silu).astype(BF16)
        for rows, start in ((here, 0), (other, half)):
            hidden[rows, :] = act[start : start + half]
            pair_back[rows, :units] = gate_back[start : start + half]
            pair_back[rows, units:] = up_back[start : start + half]
        total = dot_t(jnp.concatenate([gate_back, up_back], axis=1), pair_w[...])
        sum_even[here, :] = total[:half]
        sum_odd[here, :] = total[half:].astype(BF16)


def feed_pair(feed, cot, live, pair_w, down_w):
    rows = feed[0].shape[0]
    units = down_w.shape[0]
    out = (
        like(rows, D, BF16), like(rows, D, BF16), like(2 * rows, units, BF16),
        like(2 * rows, 2 * units, BF16), like(rows, D, F32), like(rows, D, BF16),
    )
    return whole_call(
        feed_kernel, out, (*feed, *cot, live, pair_w, down_w),
        20 * rows * D * units, 20 * rows * D,
    )


def outer_kernel(count, *refs):
    lefts, rights, out = refs[:count], refs[count:-1], refs[-1]
    ratio = count // len(rights)
    rows = lefts[0].shape[0]
    cols = out.shape[1]
    step = min(cols, 512)

    tile = min(out.shape[0], TILE)

    @pl.loop(0, out.shape[0] // tile)
    def _(m):
        part = pl.ds(pl.multiple_of(m * tile, tile), tile)
        for n in range(cols // step):
            span = slice(n * step, (n + 1) * step)
            total = None
            for k, left in enumerate(lefts):
                first = (k % ratio) * rows
                right = rights[k // ratio][first : first + rows, span]
                term = dot_outer(left[:, part], right)
                total = term if k == 0 else total + term
            out[part, span] = total.astype(BF16)


def outer_blocks(lefts, rights):
    rows = sum(left.shape[0] for left in lefts)
    wide, cols = lefts[0].shape[1], rights[0].shape[1]
    return whole_call(
        functools.partial(outer_kernel, len(lefts)), like(wide, cols, BF16), (*lefts, *rights),
        2 * rows * wide * cols, 2 * rows * (wide + cols),
    )


def cut_kernel(me, gate, up, out):
    @pl.when(pl.program_id(0) == 0)
    def _():
        out[...] = gate[...]

    @pl.when(pl.program_id(0) == 1)
    def _():
        out[...] = up[...]


def cut_columns(me, gate, up, planes, size):
    shard, ff = gate.shape
    mine = ff // planes // size
    if mine % LANES:
        cut = [
            lax.dynamic_slice_in_dim(w.reshape(shard, planes, size, mine), me, 1, 2)
            for w in (gate, up)
        ]
        return jnp.concatenate([c.reshape(shard, planes * mine) for c in cut], axis=1)
    block = pl.BlockSpec((shard, mine), lambda g, z, me_ref: (0, z * size + me_ref[0]))
    return pl.pallas_call(
        cut_kernel,
        out_shape=like(shard, 2 * planes * mine, BF16),
        grid_spec=pltpu.PrefetchScalarGridSpec(
            num_scalar_prefetch=1,
            grid=(2, planes),
            in_specs=[block, block],
            out_specs=pl.BlockSpec((shard, mine), lambda g, z, me_ref: (0, g * planes + z)),
        ),
        name="cut",
    )(me.reshape(1).astype(jnp.int32), gate, up)


def spread_kernel(order, *refs):
    size = (len(refs) - 2) // 2
    gate, up = refs[-2:]
    for r in range(size):
        cols = pl.ds(pl.multiple_of(order[r] * LANES, LANES), LANES)
        gate[:, cols] = refs[r][...].astype(F32)
        up[:, cols] = refs[size + r][...].astype(F32)


def spread_columns(begun, shape, planes, size, order):
    shard, both = shape
    mine = both // 2 // planes
    ff = both // 2 * size
    if size != 8 or mine != LANES:
        pieces = lax.all_gather(begun, "ctx", axis=0)
        wide = pieces.reshape(size, shard, 2, planes, mine).transpose(2, 1, 3, 0, 4)
        wide = wide.reshape(2, shard, ff).astype(F32)
        return wide[0], wide[1]
    pieces = [part for pair in gather_end(begun, size) for part in pair]
    out = pl.BlockSpec((shard, size * mine), lambda z, order_ref: (0, z))
    gate_in = pl.BlockSpec((shard, mine), lambda z, order_ref: (0, z))
    up_in = pl.BlockSpec((shard, mine), lambda z, order_ref: (0, planes + z))
    return pl.pallas_call(
        spread_kernel,
        out_shape=(like(shard, ff, F32), like(shard, ff, F32)),
        grid_spec=pltpu.PrefetchScalarGridSpec(
            num_scalar_prefetch=1,
            grid=(planes,),
            in_specs=[gate_in] * size + [up_in] * size,
            out_specs=(out, out),
        ),
        name="spread",
    )(order, *pieces, *pieces)


def compact_matrix(rows, cols, place):
    source = lax.broadcasted_iota(jnp.int32, (rows, cols), 0)
    target = lax.broadcasted_iota(jnp.int32, (rows, cols), 1)
    return (source == place(target)).astype(BF16)


def heads_kernel(heads, shares, pieces, query, key, value, out):
    size = pieces.shape[0]
    shard = query.shape[0]
    group = LANES * 3

    def select(parts):
        width = pieces.shape[2]
        source = lax.broadcasted_iota(jnp.int32, (width, group), 0)
        target = lax.broadcasted_iota(jnp.int32, (width, group), 1)
        total = None
        for slot, (device, start, span) in enumerate(parts):
            inside = (target >= slot * span) & (target < (slot + 1) * span)
            choose = (inside & (source == target - slot * span + start)).astype(BF16)
            part = dot(pieces[device, :shard, :], choose)
            total = part if total is None else total + part
        return total

    q_cols = heads * HEAD_WIDTH
    per = group // q_cols
    for j in range(size // per):
        parts = [(j * per + i, 0, q_cols) for i in range(per)]
        query[:, j * group : (j + 1) * group] = select(parts)
    per = group // HEAD_WIDTH
    for target, start in ((key, q_cols), (value, q_cols + HEAD_WIDTH)):
        for j in range(KEY_VALUE_HEADS // per):
            parts = [((j * per + i) * shares, start, HEAD_WIDTH) for i in range(per)]
            target[:, j * group : (j + 1) * group] = select(parts)
    rows = pieces.shape[1] - shard
    for z in range(size // 2):
        for q in range(2):
            out[q * rows : (q + 1) * rows, z * shard : (z + 1) * shard] = pieces[
                2 * z + q, shard:, :shard
            ].astype(F32)


def spread_heads(pieces, heads, shares, shard):
    kv = KEY_VALUE_HEADS * HEAD_WIDTH
    out = (like(shard, D, F32), like(shard, kv, F32), like(shard, kv, F32), like(shard, D, F32))
    return whole_call(
        functools.partial(heads_kernel, heads, shares), out, (pieces,),
        4 * shard * D * D, 8 * shard * D,
    )


def after(value, *others):
    return lax.optimization_barrier((value, *others))[0]


def hop(value, size, bit):
    return lax.ppermute(value, "ctx", [(i, i ^ bit) for i in range(size)])


def gather_begin(block, size):
    if size != 8:
        return block
    return block, hop(block, size, 2), hop(block, size, 4)


def gather_end(begun, size):
    if size != 8:
        whole = lax.all_gather(begun, "ctx", axis=0, tiled=True)
        return [tuple(jnp.split(part, 2)) for part in jnp.split(whole, CHUNKS)]
    block, across, along = begun
    half = block.shape[0] // 2
    upper = hop(along[:half], size, 2)
    lower = hop(across[half:], size, 4)
    corner = jnp.concatenate([upper, lower])
    return [(part, hop(part, size, 1)) for part in (block, across, along, corner)]


def gather_rows(block, size):
    return gather_end(gather_begin(block, size), size)


def scatter_rows(pairs, size, before_last=(), before_first=()):
    if size != 8:
        whole = jnp.concatenate([part.astype(BF16) for pair in pairs for part in pair])
        total = lax.psum_scatter(whole, "ctx", scatter_dimension=0, tiled=True).astype(F32)
        return total, total

    def fold(k):
        even, odd = pairs[k]
        return even + hop(odd.astype(BF16), size, 1).astype(F32)

    corner, across, along, own = fold(3), fold(1), fold(2), fold(0)
    half = own.shape[0] // 2

    def send(value, bit):
        return hop(value, size, bit).astype(F32)

    firsts = (corner[:half], corner[half:], across[:half], along[half:])
    firsts = tuple(value.astype(BF16) for value in firsts)
    if before_first:
        firsts = lax.optimization_barrier((*firsts, *before_first))[:4]
    for_along = send(firsts[0], 2)
    for_across = send(firsts[1], 4)
    across_top = send(firsts[2], 2)
    along_low = send(firsts[3], 4)
    across_rest = (across[half:] + for_across).astype(BF16)
    along_rest = (along[:half] + for_along).astype(BF16)
    if before_last:
        across_rest, along_rest, *_ = lax.optimization_barrier(
            (across_rest, along_rest, *before_last)
        )
    across_low = send(across_rest, 2)
    along_top = send(along_rest, 4)
    total = jnp.concatenate(
        [own[:half] + across_top + along_top, own[half:] + across_low + along_low]
    )
    return total, along_rest


def swap_planes(value, size, planes):
    moves = []
    for chip in range(size // 2):
        for core in range(2):
            for z in range(planes):
                moves.append(((chip * 2 + core) * planes + z, (z * 2 + core) * planes + chip))
    return lax.ppermute(value, ("ctx", "fsdp"), moves)


def norm_back(residual, scale_rows, gain, upstream):
    weighted = upstream * gain
    row_inner = jnp.mean(weighted * residual, axis=-1, keepdims=True)
    return scale_rows * weighted - residual * (scale_rows * scale_rows * scale_rows) * row_inner


def local(
    size,
    planes,
    tokens,
    cotangent,
    attend_gain,
    w_query,
    w_key,
    w_value,
    w_out,
    feed_gain,
    w_gate,
    w_up,
    w_down,
    lengths,
    deal_table,
):
    me = lax.axis_index("ctx")
    plane = lax.axis_index("fsdp")
    rows_here = tokens.shape[1]
    rows_all = rows_here * size
    heads = QUERY_HEADS // size
    shares = max(1, size // KEY_VALUE_HEADS)
    shard = w_query.shape[0]
    ff = w_gate.shape[1]
    ff_mine = ff // planes // size
    q_cols = heads * HEAD_WIDTH
    key_head = me // shares
    turn_cols = (heads + 1) * LANES
    piece = rows_all // CHUNKS
    rows_half = piece // 2

    turn_mine = q_cols + HEAD_WIDTH
    cut_cols = turn_mine + HEAD_WIDTH
    wide_cols = turn_cols + LANES

    def place(target):
        turned_col = (target // HALF) * (LANES // 2) + lax.rem(target, HALF)
        return jnp.where(target < turn_mine, turned_col, target - turn_mine + turn_cols)

    compact = compact_matrix(wide_cols, cut_cols, place)
    query_cut = lax.dynamic_slice_in_dim(w_query, me * q_cols, q_cols, 1)
    key_cut = lax.dynamic_slice_in_dim(w_key, key_head * HEAD_WIDTH, HEAD_WIDTH, 1)
    value_cut = lax.dynamic_slice_in_dim(w_value, key_head * HEAD_WIDTH, HEAD_WIDTH, 1)
    gains = jnp.stack([attend_gain, feed_gain])
    gains = jnp.pad(gains, ((0, 14), (0, cut_cols - shard)))
    proj_cut = jnp.concatenate([query_cut, key_cut, value_cut], axis=1)
    proj_all = lax.all_gather(jnp.concatenate([proj_cut, gains]), "fsdp", axis=0)
    gain_one = proj_all[:, shard, :shard].reshape(1, D).astype(F32)
    gain_two = proj_all[:, shard + 1, :shard].reshape(1, D).astype(F32)
    proj_w = dot_t(proj_all[:, :shard].reshape(D, cut_cols), compact).astype(BF16)
    out_piece = lax.dynamic_slice(
        w_out, (lax.rem(me, 2) * q_cols, (me // 2) * shard), (q_cols, shard)
    )
    out_piece = swap_planes(out_piece, size, planes)
    out_rows = q_cols * shard // D
    down_cut = lax.dynamic_slice_in_dim(w_down, me * ff_mine, ff_mine, 0)
    down_all = lax.all_gather(
        jnp.concatenate([down_cut, out_piece.reshape(out_rows, D)]), "fsdp", axis=0
    )
    down_w = down_all[:, :ff_mine].reshape(planes * ff_mine, D)
    out_w = down_all[:, ff_mine:].reshape(planes, q_cols, shard).transpose(1, 0, 2)
    out_w = out_w.reshape(heads, HEAD_WIDTH, D)
    out_w = jnp.pad(out_w, ((0, 0), (0, LANES - HEAD_WIDTH), (0, 0)))
    out_w = out_w.reshape(heads * LANES, D)
    pair_w = lax.all_gather(cut_columns(me, w_gate, w_up, planes, size), "fsdp", axis=0, tiled=True)
    order = jnp.arange(size, dtype=jnp.int32)
    if size == 8:
        order = jnp.bitwise_xor(order, me)
    table = deal_table.reshape(size, rows_here // BLK)[order].reshape(-1)
    pos_all = (table[:, None] * BLK + jnp.arange(BLK, dtype=jnp.int32)[None, :]).reshape(-1)
    live_all = (pos_all < lengths[0]).astype(F32)[:, None]
    if size == 8:
        live = live_all[:rows_here]
    else:
        live = lax.dynamic_slice_in_dim(live_all, me * rows_here, rows_here)
    frequency = ROPE_BASE ** (-2.0 * jnp.arange(HALF, dtype=F32) / HEAD_WIDTH)
    angles = pos_all.astype(F32)[:, None] * frequency[None, :]
    pad = jnp.zeros((rows_all, LANES // 2 - HALF), F32)
    cosine, sine = jnp.cos(angles), jnp.sin(angles)
    cos_t = jnp.concatenate([cosine, pad, cosine, pad], axis=1)
    sin_t = jnp.concatenate([-sine, pad, sine, pad], axis=1)

    def part_of(array, k):
        return array[k * piece : (k + 1) * piece]

    def project_rows(rows, weight):
        half = rows.shape[0] // 2
        odd = dot(rows[half:], weight).astype(BF16)
        return dot(rows[:half], weight), odd

    token_pairs = gather_rows(tokens[0], size)
    residual = tokens[0].astype(F32)
    scale_one = scale_of(residual)
    attend_low, raws = [], []
    for pair in token_pairs:
        even, odd, raw = project_pair(pair, proj_w, gain_one)
        attend_low += [even, odd]
        raws.append(raw)
    ctx_low, *saved = attend(table, lengths, raws, cos_t, sin_t, heads)
    attend_branch, _ = scatter_rows(
        [project_rows(part_of(ctx_low, k), out_w) for k in range(CHUNKS)], size
    )
    middle = residual + attend_branch

    cot_pairs = gather_rows(after(cotangent[0], token_pairs[1][0], token_pairs[2][0]), size)
    scale_two = scale_of(middle)
    feed_pairs = gather_rows((middle * scale_two * gain_two).astype(BF16), size)
    back_low, hidden, pair_back, sums_in = [], [], [], []
    for k in range(CHUNKS):
        low_even, low_odd, hidden_k, pair_k, sum_even, sum_odd = feed_pair(
            feed_pairs[k], cot_pairs[k], part_of(live_all, k), pair_w, down_w
        )
        back_low += [low_even, low_odd]
        hidden.append(hidden_k)
        pair_back.append(pair_k)
        sums_in.append((sum_even, sum_odd))
    pair_grad = outer_blocks([block for pair in feed_pairs for block in pair], pair_back)
    down_grad = outer_blocks(
        [h[i * rows_half : (i + 1) * rows_half] for h in hidden for i in range(2)], back_low,
    )
    back_feed_in, _ = scatter_rows(sums_in, size, (pair_grad, down_grad))
    pair_grad = lax.psum_scatter(pair_grad, "fsdp", scatter_dimension=0, tiled=True)
    down_grad = lax.psum_scatter(down_grad, "fsdp", scatter_dimension=0, tiled=True)
    back_final = cotangent[0].astype(F32) * live
    back_middle = back_final + norm_back(middle, scale_two, gain_two, back_feed_in)
    gain_two_grad = jnp.sum(back_feed_in * middle * scale_two, axis=0)

    mid_pairs = gather_rows(back_middle.astype(BF16), size)
    mid_blocks = [block for pair in mid_pairs for block in pair]
    grad_down = lax.all_gather(
        after(down_grad, mid_blocks[-1]), "ctx", axis=0, tiled=True
    ).astype(F32)
    pair_begun = gather_begin(after(pair_grad, mid_blocks[-1]), size)
    back_context = [dot_t(block, out_w).astype(BF16) for block in mid_blocks]
    turned = attend_back(table, lengths, saved, back_context, cos_t, sin_t, heads)
    if shares > 1:
        pairs = [[g * shares + i for i in range(shares)] for g in range(size // shares)]
        both = lax.psum(turned[:, heads * LANES :].astype(F32), "ctx", axis_index_groups=pairs)
        first = (lax.rem(me, shares) == 0).astype(F32)
        turned = jnp.concatenate([turned[:, : heads * LANES], (both * first).astype(BF16)], axis=1)
    sums_in, gain_sums = [], []
    for k in range(CHUNKS):
        sum_even, sum_odd, gain_sum = project_back_pair(
            part_of(turned, k), proj_w, token_pairs[k]
        )
        sums_in.append((sum_even, sum_odd))
        gain_sums.append(gain_sum)
    sums_in = lax.optimization_barrier(sums_in)
    back_attend_in, attend_sent = scatter_rows(sums_in, size)
    pair_begun = jax.tree.map(lambda value: after(value, attend_sent), pair_begun)
    grad_gate, grad_up = spread_columns(pair_begun, pair_grad.shape, planes, size, order)
    grad_tokens = back_middle + norm_back(residual, scale_one, gain_one, back_attend_in)
    gain_one_grad = (gain_sums[0] + gain_sums[1] + gain_sums[2] + gain_sums[3])[0]

    narrow = dot(turned, compact).astype(BF16)
    proj_grad = outer_blocks(attend_low, [narrow])
    late_ctx = after(ctx_low, turned)
    out_grad = outer_blocks(
        [late_ctx[i * rows_half : (i + 1) * rows_half] for i in range(2 * CHUNKS)], mid_blocks,
    )
    out_grad = out_grad.reshape(heads, LANES, planes, shard)[:, :HEAD_WIDTH]
    out_grad = out_grad.reshape(q_cols, planes, shard).transpose(1, 0, 2)
    out_grad = jnp.pad(out_grad, ((0, 0), (0, 0), (0, cut_cols - shard)))
    head_grad = jnp.concatenate([proj_grad.reshape(planes, shard, cut_cols), out_grad], axis=1)
    head_grad = lax.psum_scatter(head_grad, "fsdp", scatter_dimension=0, tiled=True)[0]
    head_grad = after(head_grad, attend_sent)
    out_piece = swap_planes(head_grad[shard:], size, planes)
    head_grad = lax.all_gather(
        jnp.concatenate([head_grad[:shard], out_piece]), "ctx", axis=0
    )
    grad_query, grad_key, grad_value, grad_out = spread_heads(head_grad, heads, shares, shard)

    parts = [project_rows(after(h, back_middle), down_w) for h in hidden]
    feed_branch, _ = scatter_rows(parts, size, (), (turned,))
    final_sum = middle + feed_branch
    layer_out = (final_sum * live).astype(BF16)
    sums = jnp.stack(
        [
            jnp.sum(final_sum * final_sum * live),
            jnp.sum(attend_branch * attend_branch * live),
            jnp.sum(feed_branch * feed_branch * live),
        ]
    )

    slot = (jnp.arange(planes) == plane).astype(F32)
    stats = jnp.pad(slot[:, None] * sums[None, :], ((0, 0), (0, LANES - 3))).reshape(-1)
    small = after(jnp.concatenate([gain_one_grad, gain_two_grad, stats]), attend_sent)
    if size == 8 and planes == 4:
        for bit in (1, 2, 4):
            small = small + hop(small, size, bit)
        for bit in (1, 2):
            small = small + lax.ppermute(small, "fsdp", [(z, z ^ bit) for z in range(planes)])
    else:
        small = lax.psum(small, ("ctx", "fsdp"))
    grad_attend_gain = lax.dynamic_slice_in_dim(small[:D], plane * shard, shard)
    grad_feed_gain = lax.dynamic_slice_in_dim(small[D : 2 * D], plane * shard, shard)
    total_sums = lax.dynamic_slice_in_dim(small[2 * D :].reshape(planes, LANES), plane, 1)[:, :3]
    rms_stats = jnp.sqrt(total_sums / (lengths.astype(F32)[:, None] * D))
    return (
        layer_out[None],
        grad_tokens[None],
        grad_attend_gain,
        grad_query,
        grad_key,
        grad_value,
        grad_out,
        grad_feed_gain,
        grad_gate,
        grad_up,
        grad_down,
        rms_stats,
    )


def solution(mesh):
    rows = P("fsdp", "ctx", None)
    vector = P("fsdp")
    matrix = P("fsdp", None)
    in_specs = (rows, rows, vector, matrix, matrix, matrix, matrix, vector, matrix, matrix, matrix)
    in_specs += (vector, P())
    out_specs = (rows, rows, vector, matrix, matrix, matrix, matrix, vector, matrix, matrix, matrix)
    out_specs += (matrix,)
    body = functools.partial(local, mesh.shape["ctx"], mesh.shape["fsdp"])


    return jax.shard_map(body, mesh=mesh, in_specs=in_specs, out_specs=out_specs, check_vma=False)
```

```python
import functools
import math

import jax
import jax.numpy as jnp
from jax import lax
from jax.experimental import pallas as pl
from jax.experimental.pallas import tpu as pltpu
from jax.sharding import PartitionSpec as P


D = 1536
QUERY_HEADS = 16
KEY_VALUE_HEADS = 8
HEAD_WIDTH = 96
HALF = HEAD_WIDTH // 2
BLK = 128
LANES = 128

EPS = 1e-05
ROPE_BASE = 10000.0
NEG = -1e30
SCALE = 1.0 / math.sqrt(HEAD_WIDTH)
TILE = 256
CHUNKS = 4

F32 = jnp.float32
BF16 = jnp.bfloat16


def dot(left, right):
    return lax.dot_general(left, right, (((1,), (0,)), ((), ())), preferred_element_type=F32)


def dot_t(left, right):
    return lax.dot_general(left, right, (((1,), (1,)), ((), ())), preferred_element_type=F32)


def dot_outer(left, right):
    return lax.dot_general(left, right, (((0,), (0,)), ((), ())), preferred_element_type=F32)


def turn(rows, cos_rows, sin_rows):
    return rows * cos_rows + pltpu.roll(rows, LANES // 2, 1) * sin_rows


def mask_tile(scores, key_start, query_start, length):
    key_pos = key_start + lax.broadcasted_iota(jnp.int32, scores.shape, 0)
    query_pos = query_start + lax.broadcasted_iota(jnp.int32, scores.shape, 1)
    return jnp.where((key_pos <= query_pos) & (key_pos < length), scores, NEG)


def attend_kernel(heads, table, length_ref, *refs):
    raws, rest = refs[:CHUNKS], refs[CHUNKS:]
    cos_t, sin_t, ctx_low, query_s, key_s, value_s, ctx_s, lse_s, value_t, score_s = rest
    rows_all = key_s.shape[0]
    piece = raws[0].shape[0] // BLK
    length = length_ref[0]

    for k, raw in enumerate(raws):

        @pl.loop(0, piece)
        def _(b, k=k, raw=raw):
            src = pl.ds(pl.multiple_of(b * BLK, BLK), BLK)
            here = pl.ds(pl.multiple_of((k * piece + b) * BLK, BLK), BLK)
            dst = pl.ds(pl.multiple_of(table[k * piece + b] * BLK, BLK), BLK)
            cos_rows = cos_t[here, :]
            sin_rows = sin_t[here, :]
            for h in range(heads):
                part = raw[src, h * LANES : (h + 1) * LANES]
                query_s[h, dst, :] = turn(part, cos_rows, sin_rows).astype(BF16)
            part = raw[src, heads * LANES : (heads + 1) * LANES]
            key_s[dst, :] = turn(part, cos_rows, sin_rows).astype(BF16)
            part = raw[src, (heads + 1) * LANES : (heads + 2) * LANES]
            value_s[dst, :] = part.astype(BF16)
            value_t[:, dst] = part.T.astype(BF16)

    every = range(heads)

    @pl.loop(0, rows_all // TILE)
    def _(i):
        q_rows = pl.ds(pl.multiple_of(i * TILE, TILE), TILE)
        full = jnp.minimum(i, length // TILE)

        def score(j, tops, masked):
            k_rows = pl.ds(pl.multiple_of(j * TILE, TILE), TILE)
            key = key_s[k_rows, :]
            out = []
            for h in every:
                tile = dot_t(key, query_s[h, q_rows, :])
                if masked:
                    tile = mask_tile(tile, j * TILE, i * TILE, length)
                score_s[h, k_rows, :] = tile
                out.append(jnp.maximum(tops[h], jnp.max(tile, axis=0, keepdims=True)))
            return tuple(out)

        tops = tuple(jnp.full((1, TILE), NEG, F32) for _ in every)
        tops = lax.fori_loop(0, full, lambda j, t: score(j, t, False), tops)
        tops = lax.fori_loop(full, i + 1, lambda j, t: score(j, t, True), tops)

        def accumulate(j, carry):
            k_rows = pl.ds(pl.multiple_of(j * TILE, TILE), TILE)
            out = []
            for h in every:
                total, context = carry[h]
                weight = jnp.exp((score_s[h, k_rows, :] - tops[h]) * SCALE)
                total = total + jnp.sum(weight, axis=0, keepdims=True)
                context = context + dot(value_t[:, k_rows], weight.astype(BF16))
                out.append((total, context))
            return tuple(out)

        start = tuple((jnp.zeros((1, TILE), F32), jnp.zeros((LANES, TILE), F32)) for _ in every)
        sums = lax.fori_loop(0, i + 1, accumulate, start)
        for h in every:
            total, context = sums[h]
            ctx_s[q_rows, h * LANES : (h + 1) * LANES] = (context / total).T
            lse_s[h, :, q_rows] = jnp.broadcast_to(tops[h] * SCALE + jnp.log(total), (8, TILE))

    @pl.loop(0, rows_all // BLK)
    def _(b):
        dst = pl.ds(pl.multiple_of(b * BLK, BLK), BLK)
        src = pl.ds(pl.multiple_of(table[b] * BLK, BLK), BLK)
        ctx_low[dst, :] = ctx_s[src, :].astype(BF16)


def attend(table, length, raws, cos_t, sin_t, heads):
    rows_all = cos_t.shape[0]
    smem = pl.BlockSpec(memory_space=pltpu.SMEM)
    vmem = pl.BlockSpec(memory_space=pltpu.VMEM)
    pairs = heads * rows_all * rows_all // 2
    return pl.pallas_call(
        functools.partial(attend_kernel, heads),
        out_shape=(
            jax.ShapeDtypeStruct((rows_all, heads * LANES), BF16),
            jax.ShapeDtypeStruct((heads, rows_all, LANES), BF16),
            jax.ShapeDtypeStruct((rows_all, LANES), BF16),
            jax.ShapeDtypeStruct((rows_all, LANES), BF16),
            jax.ShapeDtypeStruct((rows_all, heads * LANES), F32),
            jax.ShapeDtypeStruct((heads, 8, rows_all), F32),
        ),
        in_specs=[smem, smem] + [vmem] * (CHUNKS + 2),
        out_specs=(vmem,) * 6,
        scratch_shapes=[
            pltpu.VMEM((LANES, rows_all), BF16),
            pltpu.VMEM((heads, rows_all, TILE), F32),
        ],
        compiler_params=pltpu.CompilerParams(vmem_limit_bytes=48 << 20),
        cost_estimate=pl.CostEstimate(
            flops=4 * pairs * LANES, transcendentals=pairs, bytes_accessed=rows_all * 8192
        ),
        name="attend",
    )(table, length, *raws, cos_t, sin_t)


def attend_back_kernel(heads, table, length_ref, query_s, key_s, value_s, ctx_s, lse_s, *refs):
    backs, rest = refs[: 2 * CHUNKS], refs[2 * CHUNKS :]
    cos_t, sin_t, out, back_s, delta_s, key_t, query_acc, key_all, value_all = rest
    rows_all = key_s.shape[0]
    piece = backs[0].shape[0] // BLK
    length = length_ref[0]
    tiles = rows_all // TILE

    for k, back_low in enumerate(backs):

        @pl.loop(0, piece)
        def _(b, k=k, back_low=back_low):
            src = pl.ds(pl.multiple_of(b * BLK, BLK), BLK)
            dst = pl.ds(pl.multiple_of(table[k * piece + b] * BLK, BLK), BLK)
            for h in range(heads):
                cols = slice(h * LANES, (h + 1) * LANES)
                part = back_low[src, cols]
                back_s[h, dst, :] = part
                inner = jnp.sum(part.astype(F32) * ctx_s[dst, cols], axis=1, keepdims=True)
                delta_s[h, :, dst] = jnp.broadcast_to(inner, (BLK, BLK)).T[:8, :]

    @pl.loop(0, rows_all // BLK)
    def _(b):
        rows = pl.ds(pl.multiple_of(b * BLK, BLK), BLK)
        key_t[:, rows] = key_s[rows, :].astype(F32).T.astype(BF16)

    query_acc[...] = jnp.zeros_like(query_acc)
    key_all[...] = jnp.zeros_like(key_all)
    value_all[...] = jnp.zeros_like(value_all)

    def step(i, j, masked):
        k_rows = pl.ds(pl.multiple_of(j * TILE, TILE), TILE)
        q_rows = pl.ds(pl.multiple_of(i * TILE, TILE), TILE)
        key = key_s[k_rows, :]
        value = value_s[k_rows, :]
        value_sum = key_sum = None
        for h in range(heads):
            query = query_s[h, q_rows, :]
            back = back_s[h, q_rows, :]
            tile = dot_t(key, query)
            if masked:
                tile = mask_tile(tile, j * TILE, i * TILE, length)
            soft = jnp.exp(tile * SCALE - lse_s[h, :1, q_rows])
            back_soft = dot_t(value, back)
            low = (soft * (back_soft - delta_s[h, :1, q_rows])).astype(BF16)
            value_part = dot(soft.astype(BF16), back)
            key_part = dot(low, query)
            value_sum = value_part if h == 0 else value_sum + value_part
            key_sum = key_part if h == 0 else key_sum + key_part
            query_acc[h, :, q_rows] += dot(key_t[:, k_rows], low)
        value_all[k_rows, :] += value_sum
        key_all[k_rows, :] += key_sum

    @pl.loop(0, tiles)
    def _(i):
        full = jnp.minimum(i, length // TILE)

        @pl.loop(0, full)
        def _(j):
            step(i, j, False)

        @pl.loop(full, i + 1)
        def _(j):
            step(i, j, True)

    @pl.loop(0, rows_all // BLK)
    def _(b):
        dst = pl.ds(pl.multiple_of(b * BLK, BLK), BLK)
        src = pl.ds(pl.multiple_of(table[b] * BLK, BLK), BLK)
        cos_rows = cos_t[dst, :]
        sin_rows = -sin_t[dst, :]
        for h in range(heads):
            part = query_acc[h, :, src].T * SCALE
            out[dst, h * LANES : (h + 1) * LANES] = turn(part, cos_rows, sin_rows).astype(BF16)
        part = key_all[src, :] * SCALE
        out[dst, heads * LANES : (heads + 1) * LANES] = turn(part, cos_rows, sin_rows).astype(BF16)
        out[dst, (heads + 1) * LANES : (heads + 2) * LANES] = value_all[src, :].astype(BF16)


def attend_back(table, length, saved, backs, cos_t, sin_t, heads):
    query_s, key_s, value_s, ctx_s, lse_s = saved
    rows_all = key_s.shape[0]
    smem = pl.BlockSpec(memory_space=pltpu.SMEM)
    vmem = pl.BlockSpec(memory_space=pltpu.VMEM)
    pairs = heads * rows_all * rows_all // 2
    return pl.pallas_call(
        functools.partial(attend_back_kernel, heads),
        out_shape=jax.ShapeDtypeStruct((rows_all, (heads + 2) * LANES), BF16),
        in_specs=[smem, smem] + [vmem] * (7 + 2 * CHUNKS),
        out_specs=vmem,
        scratch_shapes=[
            pltpu.VMEM((heads, rows_all, LANES), BF16),
            pltpu.VMEM((heads, 8, rows_all), F32),
            pltpu.VMEM((LANES, rows_all), BF16),
            pltpu.VMEM((heads, LANES, rows_all), F32),
            pltpu.VMEM((rows_all, LANES), F32),
            pltpu.VMEM((rows_all, LANES), F32),
        ],
        compiler_params=pltpu.CompilerParams(vmem_limit_bytes=48 << 20),
        cost_estimate=pl.CostEstimate(
            flops=10 * pairs * LANES, transcendentals=pairs, bytes_accessed=rows_all * 8192
        ),
        name="attend_back",
    )(table, length, query_s, key_s, value_s, ctx_s, lse_s, *backs, cos_t, sin_t)


def whole_call(kernel, out_shape, args, flops, nbytes):
    vmem = pl.BlockSpec(memory_space=pltpu.VMEM)
    return pl.pallas_call(
        kernel,
        out_shape=out_shape,
        in_specs=[vmem] * len(args),
        out_specs=jax.tree.map(lambda _: vmem, out_shape),
        compiler_params=pltpu.CompilerParams(vmem_limit_bytes=48 << 20),
        cost_estimate=pl.CostEstimate(flops=flops, transcendentals=0, bytes_accessed=nbytes),
    )(*args)


def like(rows, cols, dtype):
    return jax.ShapeDtypeStruct((rows, cols), dtype)


def scale_of(rows):
    return lax.rsqrt(jnp.mean(rows * rows, axis=-1, keepdims=True) + EPS)


def project_kernel(even, odd, weight, gain, low_even, low_odd, raw):
    for source, low, start in ((even, low_even, 0), (odd, low_odd, even.shape[0])):
        for b in range(source.shape[0] // TILE):
            src = slice(b * TILE, (b + 1) * TILE)
            rows_f = source[src, :].astype(F32)
            low[src, :] = (rows_f * scale_of(rows_f) * gain[...]).astype(BF16)
            raw[start + b * TILE : start + (b + 1) * TILE, :] = dot(low[src, :], weight[...])


def project_pair(pair, weight, gain):
    rows = pair[0].shape[0]
    cols = weight.shape[1]
    out = (like(rows, D, BF16), like(rows, D, BF16), like(2 * rows, cols, F32))
    return whole_call(project_kernel, out, (*pair, weight, gain), 4 * rows * D * cols, 8 * rows * D)


def project_back_kernel(turned, weight, even, odd, sum_even, sum_odd, gain_sum):
    total = jnp.zeros((1, D), F32)
    for tokens, out, start in ((odd, sum_odd, even.shape[0]), (even, sum_even, 0)):
        for b in range(tokens.shape[0] // TILE):
            dst = slice(b * TILE, (b + 1) * TILE)
            rows_f = tokens[dst, :].astype(F32)
            part = dot_t(turned[start + b * TILE : start + (b + 1) * TILE, :], weight[...])
            out[dst, :] = part.astype(out.dtype)
            total = total + jnp.sum(part * rows_f * scale_of(rows_f), axis=0, keepdims=True)
    gain_sum[...] = jnp.broadcast_to(total, gain_sum.shape)


def project_back_pair(turned, weight, pair):
    rows = pair[0].shape[0]
    cols = weight.shape[1]
    out = (like(rows, D, F32), like(rows, D, BF16), like(8, D, F32))
    return whole_call(
        project_back_kernel, out, (turned, weight, *pair),
        4 * rows * D * cols, 10 * rows * D,
    )


def feed_kernel(
    feed_even, feed_odd, cot_even, cot_odd, live, pair_w, down_w, low_even, low_odd, hidden,
    pair_back, sum_even, sum_odd,
):
    units = down_w.shape[0]
    half = TILE
    for b in range(feed_even.shape[0] // half):
        here = slice(b * half, (b + 1) * half)
        other = slice(feed_even.shape[0] + b * half, feed_even.shape[0] + (b + 1) * half)
        low_even[here, :] = (cot_even[here, :].astype(F32) * live[here, :]).astype(BF16)
        low_odd[here, :] = (cot_odd[here, :].astype(F32) * live[other, :]).astype(BF16)
        feed = jnp.concatenate([feed_even[here, :], feed_odd[here, :]])
        low = jnp.concatenate([low_even[here, :], low_odd[here, :]])
        gate_pre = dot(feed, pair_w[:, :units])
        up_pre = dot(feed, pair_w[:, units:])
        back_hidden = dot_t(low, down_w[...])
        gate_sigmoid = jax.nn.sigmoid(gate_pre)
        gate_silu = gate_pre * gate_sigmoid
        act = (gate_silu * up_pre).astype(BF16)
        gate_back = (
            back_hidden * up_pre * gate_sigmoid * (1.0 + gate_pre * (1.0 - gate_sigmoid))
        ).astype(BF16)
        up_back = (back_hidden * gate_silu).astype(BF16)
        for rows, start in ((here, 0), (other, half)):
            hidden[rows, :] = act[start : start + half]
            pair_back[rows, :units] = gate_back[start : start + half]
            pair_back[rows, units:] = up_back[start : start + half]
        total = dot_t(jnp.concatenate([gate_back, up_back], axis=1), pair_w[...])
        sum_even[here, :] = total[:half]
        sum_odd[here, :] = total[half:].astype(BF16)


def feed_pair(feed, cot, live, pair_w, down_w):
    rows = feed[0].shape[0]
    units = down_w.shape[0]
    out = (
        like(rows, D, BF16), like(rows, D, BF16), like(2 * rows, units, BF16),
        like(2 * rows, 2 * units, BF16), like(rows, D, F32), like(rows, D, BF16),
    )
    return whole_call(
        feed_kernel, out, (*feed, *cot, live, pair_w, down_w),
        20 * rows * D * units, 20 * rows * D,
    )


def outer_kernel(count, *refs):
    lefts, rights, out = refs[:count], refs[count:-1], refs[-1]
    ratio = count // len(rights)
    rows = lefts[0].shape[0]
    cols = out.shape[1]
    step = min(cols, 512)

    tile = min(out.shape[0], TILE)

    @pl.loop(0, out.shape[0] // tile)
    def _(m):
        part = pl.ds(pl.multiple_of(m * tile, tile), tile)
        for n in range(cols // step):
            span = slice(n * step, (n + 1) * step)
            total = None
            for k, left in enumerate(lefts):
                first = (k % ratio) * rows
                right = rights[k // ratio][first : first + rows, span]
                term = dot_outer(left[:, part], right)
                total = term if k == 0 else total + term
            out[part, span] = total.astype(BF16)


def outer_blocks(lefts, rights):
    rows = sum(left.shape[0] for left in lefts)
    wide, cols = lefts[0].shape[1], rights[0].shape[1]
    return whole_call(
        functools.partial(outer_kernel, len(lefts)), like(wide, cols, BF16), (*lefts, *rights),
        2 * rows * wide * cols, 2 * rows * (wide + cols),
    )


def cut_kernel(me, gate, up, out):
    @pl.when(pl.program_id(0) == 0)
    def _():
        out[...] = gate[...]

    @pl.when(pl.program_id(0) == 1)
    def _():
        out[...] = up[...]


def cut_columns(me, gate, up, planes, size):
    shard, ff = gate.shape
    mine = ff // planes // size
    if mine % LANES:
        cut = [
            lax.dynamic_slice_in_dim(w.reshape(shard, planes, size, mine), me, 1, 2)
            for w in (gate, up)
        ]
        return jnp.concatenate([c.reshape(shard, planes * mine) for c in cut], axis=1)
    block = pl.BlockSpec((shard, mine), lambda g, z, me_ref: (0, z * size + me_ref[0]))
    return pl.pallas_call(
        cut_kernel,
        out_shape=like(shard, 2 * planes * mine, BF16),
        grid_spec=pltpu.PrefetchScalarGridSpec(
            num_scalar_prefetch=1,
            grid=(2, planes),
            in_specs=[block, block],
            out_specs=pl.BlockSpec((shard, mine), lambda g, z, me_ref: (0, g * planes + z)),
        ),
        name="cut",
    )(me.reshape(1).astype(jnp.int32), gate, up)


def spread_kernel(order, *refs):
    size = (len(refs) - 2) // 2
    gate, up = refs[-2:]
    for r in range(size):
        cols = pl.ds(pl.multiple_of(order[r] * LANES, LANES), LANES)
        gate[:, cols] = refs[r][...].astype(F32)
        up[:, cols] = refs[size + r][...].astype(F32)


def spread_columns(begun, shape, planes, size, order):
    shard, both = shape
    mine = both // 2 // planes
    ff = both // 2 * size
    if size != 8 or mine != LANES:
        pieces = lax.all_gather(begun, "ctx", axis=0)
        wide = pieces.reshape(size, shard, 2, planes, mine).transpose(2, 1, 3, 0, 4)
        wide = wide.reshape(2, shard, ff).astype(F32)
        return wide[0], wide[1]
    pieces = [part for pair in gather_end(begun, size) for part in pair]
    out = pl.BlockSpec((shard, size * mine), lambda z, order_ref: (0, z))
    gate_in = pl.BlockSpec((shard, mine), lambda z, order_ref: (0, z))
    up_in = pl.BlockSpec((shard, mine), lambda z, order_ref: (0, planes + z))
    return pl.pallas_call(
        spread_kernel,
        out_shape=(like(shard, ff, F32), like(shard, ff, F32)),
        grid_spec=pltpu.PrefetchScalarGridSpec(
            num_scalar_prefetch=1,
            grid=(planes,),
            in_specs=[gate_in] * size + [up_in] * size,
            out_specs=(out, out),
        ),
        name="spread",
    )(order, *pieces, *pieces)


def compact_matrix(rows, cols, place):
    source = lax.broadcasted_iota(jnp.int32, (rows, cols), 0)
    target = lax.broadcasted_iota(jnp.int32, (rows, cols), 1)
    return (source == place(target)).astype(BF16)


def heads_kernel(heads, shares, pieces, query, key, value, out):
    size = pieces.shape[0]
    shard = query.shape[0]
    group = LANES * 3

    def select(parts):
        width = pieces.shape[2]
        source = lax.broadcasted_iota(jnp.int32, (width, group), 0)
        target = lax.broadcasted_iota(jnp.int32, (width, group), 1)
        total = None
        for slot, (device, start, span) in enumerate(parts):
            inside = (target >= slot * span) & (target < (slot + 1) * span)
            choose = (inside & (source == target - slot * span + start)).astype(BF16)
            part = dot(pieces[device, :shard, :], choose)
            total = part if total is None else total + part
        return total

    q_cols = heads * HEAD_WIDTH
    per = group // q_cols
    for j in range(size // per):
        parts = [(j * per + i, 0, q_cols) for i in range(per)]
        query[:, j * group : (j + 1) * group] = select(parts)
    per = group // HEAD_WIDTH
    for target, start in ((key, q_cols), (value, q_cols + HEAD_WIDTH)):
        for j in range(KEY_VALUE_HEADS // per):
            parts = [((j * per + i) * shares, start, HEAD_WIDTH) for i in range(per)]
            target[:, j * group : (j + 1) * group] = select(parts)
    rows = pieces.shape[1] - shard
    for z in range(size // 2):
        for q in range(2):
            out[q * rows : (q + 1) * rows, z * shard : (z + 1) * shard] = pieces[
                2 * z + q, shard:, :shard
            ].astype(F32)


def spread_heads(pieces, heads, shares, shard):
    kv = KEY_VALUE_HEADS * HEAD_WIDTH
    out = (like(shard, D, F32), like(shard, kv, F32), like(shard, kv, F32), like(shard, D, F32))
    return whole_call(
        functools.partial(heads_kernel, heads, shares), out, (pieces,),
        4 * shard * D * D, 8 * shard * D,
    )


def after(value, *others):
    return lax.optimization_barrier((value, *others))[0]


def hop(value, size, bit):
    return lax.ppermute(value, "ctx", [(i, i ^ bit) for i in range(size)])


def gather_begin(block, size):
    if size != 8:
        return block
    return block, hop(block, size, 2), hop(block, size, 4)


def gather_end(begun, size):
    if size != 8:
        whole = lax.all_gather(begun, "ctx", axis=0, tiled=True)
        return [tuple(jnp.split(part, 2)) for part in jnp.split(whole, CHUNKS)]
    block, across, along = begun
    half = block.shape[0] // 2
    upper = hop(along[:half], size, 2)
    lower = hop(across[half:], size, 4)
    corner = jnp.concatenate([upper, lower])
    return [(part, hop(part, size, 1)) for part in (block, across, along, corner)]


def gather_rows(block, size):
    return gather_end(gather_begin(block, size), size)


def scatter_rows(pairs, size, before_last=(), before_first=()):
    if size != 8:
        whole = jnp.concatenate([part.astype(BF16) for pair in pairs for part in pair])
        total = lax.psum_scatter(whole, "ctx", scatter_dimension=0, tiled=True).astype(F32)
        return total, (total,)

    def fold(k):
        even, odd = pairs[k]
        return even + hop(odd.astype(BF16), size, 1).astype(F32)

    corner, across, along, own = fold(3), fold(1), fold(2), fold(0)
    half = own.shape[0] // 2

    def send(value, bit):
        return hop(value, size, bit).astype(F32)

    firsts = (corner[:half], corner[half:], across[:half], along[half:])
    firsts = tuple(value.astype(BF16) for value in firsts)
    if before_first:
        firsts = lax.optimization_barrier((*firsts, *before_first))[:4]
    for_along = send(firsts[0], 2)
    for_across = send(firsts[1], 4)
    across_top = send(firsts[2], 2)
    along_low = send(firsts[3], 4)
    across_rest = (across[half:] + for_across).astype(BF16)
    along_rest = (along[:half] + for_along).astype(BF16)
    if before_last:
        across_rest, along_rest, *_ = lax.optimization_barrier(
            (across_rest, along_rest, *before_last)
        )
    across_low = send(across_rest, 2)
    along_top = send(along_rest, 4)
    total = jnp.concatenate(
        [own[:half] + across_top + along_top, own[half:] + across_low + along_low]
    )
    return total, (along_rest, across_rest, across_top, along_low)


def swap_planes(value, size, planes):
    moves = []
    for chip in range(size // 2):
        for core in range(2):
            for z in range(planes):
                moves.append(((chip * 2 + core) * planes + z, (z * 2 + core) * planes + chip))
    return lax.ppermute(value, ("ctx", "fsdp"), moves)


def norm_back(residual, scale_rows, gain, upstream):
    weighted = upstream * gain
    row_inner = jnp.mean(weighted * residual, axis=-1, keepdims=True)
    return scale_rows * weighted - residual * (scale_rows * scale_rows * scale_rows) * row_inner


def local(
    size,
    planes,
    tokens,
    cotangent,
    attend_gain,
    w_query,
    w_key,
    w_value,
    w_out,
    feed_gain,
    w_gate,
    w_up,
    w_down,
    lengths,
    deal_table,
):
    me = lax.axis_index("ctx")
    plane = lax.axis_index("fsdp")
    rows_here = tokens.shape[1]
    rows_all = rows_here * size
    heads = QUERY_HEADS // size
    shares = max(1, size // KEY_VALUE_HEADS)
    shard = w_query.shape[0]
    ff = w_gate.shape[1]
    ff_mine = ff // planes // size
    q_cols = heads * HEAD_WIDTH
    key_head = me // shares
    turn_cols = (heads + 1) * LANES
    piece = rows_all // CHUNKS
    rows_half = piece // 2

    turn_mine = q_cols + HEAD_WIDTH
    cut_cols = turn_mine + HEAD_WIDTH
    wide_cols = turn_cols + LANES

    def place(target):
        turned_col = (target // HALF) * (LANES // 2) + lax.rem(target, HALF)
        return jnp.where(target < turn_mine, turned_col, target - turn_mine + turn_cols)

    compact = compact_matrix(wide_cols, cut_cols, place)
    query_cut = lax.dynamic_slice_in_dim(w_query, me * q_cols, q_cols, 1)
    key_cut = lax.dynamic_slice_in_dim(w_key, key_head * HEAD_WIDTH, HEAD_WIDTH, 1)
    value_cut = lax.dynamic_slice_in_dim(w_value, key_head * HEAD_WIDTH, HEAD_WIDTH, 1)
    gains = jnp.stack([attend_gain, feed_gain])
    gains = jnp.pad(gains, ((0, 14), (0, cut_cols - shard)))
    proj_cut = jnp.concatenate([query_cut, key_cut, value_cut], axis=1)
    proj_all = lax.all_gather(jnp.concatenate([proj_cut, gains]), "fsdp", axis=0)
    gain_one = proj_all[:, shard, :shard].reshape(1, D).astype(F32)
    gain_two = proj_all[:, shard + 1, :shard].reshape(1, D).astype(F32)
    proj_w = dot_t(proj_all[:, :shard].reshape(D, cut_cols), compact).astype(BF16)
    out_piece = lax.dynamic_slice(
        w_out, (lax.rem(me, 2) * q_cols, (me // 2) * shard), (q_cols, shard)
    )
    out_piece = swap_planes(out_piece, size, planes)
    down_cut = lax.dynamic_slice_in_dim(w_down, me * ff_mine, ff_mine, 0)
    blocks = [down_cut[:, z * shard : (z + 1) * shard] for z in range(planes)]
    down_all = lax.all_gather(jnp.concatenate([*blocks, out_piece]), "fsdp", axis=0)
    down_rows = planes * ff_mine
    down_w = down_all[:, :down_rows].reshape(planes, planes, ff_mine, shard)
    down_w = down_w.transpose(0, 2, 1, 3).reshape(down_rows, D)
    out_w = down_all[:, down_rows:].transpose(1, 0, 2).reshape(q_cols, D)
    out_w = out_w.reshape(heads, HEAD_WIDTH, D)
    out_w = jnp.pad(out_w, ((0, 0), (0, LANES - HEAD_WIDTH), (0, 0)))
    out_w = out_w.reshape(heads * LANES, D)
    pair_cut = cut_columns(me, w_gate, w_up, planes, size)
    pair_w = lax.all_gather(pair_cut, "fsdp", axis=0, tiled=True)
    order = jnp.arange(size, dtype=jnp.int32)
    if size == 8:
        order = jnp.bitwise_xor(order, me)
    table = deal_table.reshape(size, rows_here // BLK)[order].reshape(-1)
    pos_all = (table[:, None] * BLK + jnp.arange(BLK, dtype=jnp.int32)[None, :]).reshape(-1)
    live_all = (pos_all < lengths[0]).astype(F32)[:, None]
    if size == 8:
        live = live_all[:rows_here]
    else:
        live = lax.dynamic_slice_in_dim(live_all, me * rows_here, rows_here)
    frequency = ROPE_BASE ** (-2.0 * jnp.arange(HALF, dtype=F32) / HEAD_WIDTH)
    angles = pos_all.astype(F32)[:, None] * frequency[None, :]
    pad = jnp.zeros((rows_all, LANES // 2 - HALF), F32)
    cosine, sine = jnp.cos(angles), jnp.sin(angles)
    cos_t = jnp.concatenate([cosine, pad, cosine, pad], axis=1)
    sin_t = jnp.concatenate([-sine, pad, sine, pad], axis=1)

    def part_of(array, k):
        return array[k * piece : (k + 1) * piece]

    def project_rows(rows, weight):
        half = rows.shape[0] // 2
        odd = dot(rows[half:], weight).astype(BF16)
        return dot(rows[:half], weight), odd

    begun = gather_begin(tokens[0], size)
    if size == 8:
        begun = (begun[0], *lax.optimization_barrier((*begun[1:], pair_cut))[:2])
    token_pairs = gather_end(begun, size)
    residual = tokens[0].astype(F32)
    scale_one = scale_of(residual)
    attend_low, raws = [], []
    for pair in token_pairs:
        even, odd, raw = project_pair(pair, proj_w, gain_one)
        attend_low += [even, odd]
        raws.append(raw)
    ctx_low, *saved = attend(table, lengths, raws, cos_t, sin_t, heads)
    attend_branch, _ = scatter_rows(
        [project_rows(part_of(ctx_low, k), out_w) for k in range(CHUNKS)], size
    )
    middle = residual + attend_branch

    cot_pairs = gather_rows(after(cotangent[0], token_pairs[3][0]), size)
    scale_two = scale_of(middle)
    feed_pairs = gather_rows((middle * scale_two * gain_two).astype(BF16), size)
    back_low, hidden, pair_back, sums_in = [], [], [], []
    for k in range(CHUNKS):
        low_even, low_odd, hidden_k, pair_k, sum_even, sum_odd = feed_pair(
            feed_pairs[k], cot_pairs[k], part_of(live_all, k), pair_w, down_w
        )
        back_low += [low_even, low_odd]
        hidden.append(hidden_k)
        pair_back.append(pair_k)
        sums_in.append((sum_even, sum_odd))
    pair_grad = outer_blocks([block for pair in feed_pairs for block in pair], pair_back)
    down_grad = outer_blocks(
        [h[i * rows_half : (i + 1) * rows_half] for h in hidden for i in range(2)], back_low,
    )
    back_feed_in, _ = scatter_rows(sums_in, size, (pair_grad, down_grad))
    pair_grad = lax.psum_scatter(pair_grad, "fsdp", scatter_dimension=0, tiled=True)
    down_grad = lax.psum_scatter(down_grad, "fsdp", scatter_dimension=0, tiled=True)
    back_final = cotangent[0].astype(F32) * live
    back_middle = back_final + norm_back(middle, scale_two, gain_two, back_feed_in)
    gain_two_grad = jnp.sum(back_feed_in * middle * scale_two, axis=0)

    mid_pairs = gather_rows(back_middle.astype(BF16), size)
    mid_blocks = [block for pair in mid_pairs for block in pair]
    grad_down = lax.all_gather(
        after(down_grad, mid_blocks[-1]), "ctx", axis=0, tiled=True
    ).astype(F32)
    pair_begun = gather_begin(after(pair_grad, mid_blocks[-1]), size)
    back_context = [dot_t(block, out_w).astype(BF16) for block in mid_blocks]
    turned = attend_back(table, lengths, saved, back_context, cos_t, sin_t, heads)
    if shares > 1:
        pairs = [[g * shares + i for i in range(shares)] for g in range(size // shares)]
        both = lax.psum(turned[:, heads * LANES :].astype(F32), "ctx", axis_index_groups=pairs)
        first = (lax.rem(me, shares) == 0).astype(F32)
        turned = jnp.concatenate([turned[:, : heads * LANES], (both * first).astype(BF16)], axis=1)
    sums_in, gain_sums = [], []
    for k in range(CHUNKS):
        sum_even, sum_odd, gain_sum = project_back_pair(
            part_of(turned, k), proj_w, token_pairs[k]
        )
        sums_in.append((sum_even, sum_odd))
        gain_sums.append(gain_sum)
    sums_in = lax.optimization_barrier(sums_in)
    back_attend_in, attend_sent = scatter_rows(sums_in, size, (), (turned,))
    pair_begun = jax.tree.map(lambda value: after(value, *attend_sent), pair_begun)
    grad_gate, grad_up = spread_columns(pair_begun, pair_grad.shape, planes, size, order)
    grad_tokens = back_middle + norm_back(residual, scale_one, gain_one, back_attend_in)
    gain_one_grad = (gain_sums[0] + gain_sums[1] + gain_sums[2] + gain_sums[3])[0]

    narrow = dot(turned, compact).astype(BF16)
    proj_grad = outer_blocks(attend_low, [narrow])
    late_ctx = after(ctx_low, turned)
    out_grad = outer_blocks(
        [late_ctx[i * rows_half : (i + 1) * rows_half] for i in range(2 * CHUNKS)], mid_blocks,
    )
    out_grad = out_grad.reshape(heads, LANES, planes, shard)[:, :HEAD_WIDTH]
    out_grad = out_grad.reshape(q_cols, planes, shard).transpose(1, 0, 2)
    out_grad = jnp.pad(out_grad, ((0, 0), (0, 0), (0, cut_cols - shard)))
    head_grad = jnp.concatenate([proj_grad.reshape(planes, shard, cut_cols), out_grad], axis=1)
    head_grad = lax.psum_scatter(head_grad, "fsdp", scatter_dimension=0, tiled=True)[0]
    head_grad = after(head_grad, *attend_sent)
    out_piece = swap_planes(head_grad[shard:], size, planes)
    head_grad = lax.all_gather(
        jnp.concatenate([head_grad[:shard], out_piece]), "ctx", axis=0
    )
    grad_query, grad_key, grad_value, grad_out = spread_heads(head_grad, heads, shares, shard)

    late = [after(hidden[0], *attend_sent)] + [after(h, back_middle) for h in hidden[1:]]
    parts = [project_rows(h, down_w) for h in late]
    feed_branch, _ = scatter_rows(parts, size, (), (turned,))
    final_sum = middle + feed_branch
    layer_out = (final_sum * live).astype(BF16)
    sums = jnp.stack(
        [
            jnp.sum(final_sum * final_sum * live),
            jnp.sum(attend_branch * attend_branch * live),
            jnp.sum(feed_branch * feed_branch * live),
        ]
    )

    slot = (jnp.arange(planes) == plane).astype(F32)
    stats = jnp.pad(slot[:, None] * sums[None, :], ((0, 0), (0, LANES - 3))).reshape(-1)
    small = after(jnp.concatenate([gain_one_grad, gain_two_grad, stats]), *attend_sent)
    if size == 8 and planes == 4:
        for bit in (1, 2, 4):
            small = small + hop(small, size, bit)
        for bit in (1, 2):
            small = small + lax.ppermute(small, "fsdp", [(z, z ^ bit) for z in range(planes)])
    else:
        small = lax.psum(small, ("ctx", "fsdp"))
    grad_attend_gain = lax.dynamic_slice_in_dim(small[:D], plane * shard, shard)
    grad_feed_gain = lax.dynamic_slice_in_dim(small[D : 2 * D], plane * shard, shard)
    total_sums = lax.dynamic_slice_in_dim(small[2 * D :].reshape(planes, LANES), plane, 1)[:, :3]
    rms_stats = jnp.sqrt(total_sums / (lengths.astype(F32)[:, None] * D))
    return (
        layer_out[None],
        grad_tokens[None],
        grad_attend_gain,
        grad_query,
        grad_key,
        grad_value,
        grad_out,
        grad_feed_gain,
        grad_gate,
        grad_up,
        grad_down,
        rms_stats,
    )


def solution(mesh):
    rows = P("fsdp", "ctx", None)
    vector = P("fsdp")
    matrix = P("fsdp", None)
    in_specs = (rows, rows, vector, matrix, matrix, matrix, matrix, vector, matrix, matrix, matrix)
    in_specs += (vector, P())
    out_specs = (rows, rows, vector, matrix, matrix, matrix, matrix, vector, matrix, matrix, matrix)
    out_specs += (matrix,)
    body = functools.partial(local, mesh.shape["ctx"], mesh.shape["fsdp"])


    return jax.shard_map(body, mesh=mesh, in_specs=in_specs, out_specs=out_specs, check_vma=False)
```
